32 devices in a mesh: slab: 2 (over y), ma: 4 (over z), freq: 2 (over x), pol: 2 (over core).
Axes of the slice: x: 2, y: 2, z: 4, core: 2. Of those that a mesh axis runs over, the one named last changes fastest.
Arguments:
- visibility: bfloat16 [16, 2, 64, 8192], P(('slab', 'freq'), None, 'pol', 'ma'), parts along dimension 0, may hold values from -6 to 6
- beam_rows: bfloat16 [16, 64, 768], P(('slab', 'freq'), 'pol'), parts along dimension 0, may hold values from -0.4375 to 0.4375
- mode_gain: float32 [192, 768], P('ma'), may hold values from 0.7 to 1.5
- harmonic_basis: bfloat16 [768, 768], replicated, may hold values from -0.21875 to 0.21875
- step_size: float32 [16], P(('slab', 'freq')), parts along dimension 0, may hold values from 0.15 to 0.25
- kl_matrix: bfloat16 [4, 8], P('slab'), parts along dimension 0, may hold values from -2 to 2
Outputs:
- filtered: bfloat16 [192, 4, 2, 768], P('ma', ('slab', 'freq'), 'pol'), parts along dimension 1
The draws below stay inside these ranges and needn't reach their ends.
There are 2 independent parts, one for each index of `slab`. The reference program is written for one: setup_inputs(seed, part) draws one part's arguments, and reference() takes and returns one part's arrays. A program takes and returns all parts, laid end to end along the dimension named above; an argument that names none is the same for every part. Nothing has to cross between parts.
All inputs are finite; a program needn't handle non-finite values.
Results may differ from the reference program's by a relative error of at most 0.0088.
Values may be sent and summed in bfloat16 or wider, within the bound.
No kernel may reach another device: no remote copies, remote signals or barrier semaphores. Data moves between devices by JAX's collectives and lax.ppermute only.
A program may use at most 64 MiB of HBM per device.

```python
import math
import jax
import jax.numpy as jnp

NT = 8192
L = 768
M = 192
FREQS = 8
KEEP = 2
BASE = 64
ITERS = 2


def levels(key, extent, cuts, low, largest):
    level, own = 1.0, jax.random.fold_in(key, 6)
    for dim, parts in cuts:
        steps = jnp.exp(jax.random.uniform(jax.random.fold_in(own, dim), (parts,), jnp.float32, low / len(cuts), largest / len(cuts)))
        level = level * jnp.repeat(steps, extent[dim] // parts).reshape([-1 if axis == dim else 1 for axis in range(len(extent))])
    return level


def gaussian(rng, shape, spread, most, shards=(), kind=jnp.bfloat16):
    values = jax.random.normal(rng, shape, jnp.float32) * spread
    if len(shards) > 0:
        values = levels(rng, shape, shards, -0.22, 0.18) * values
    return jnp.clip(values, min=-most, max=most).astype(kind)


def setup_inputs(seed: int = 0, part: int = 0) -> dict:
    keys = jax.random.split(jax.random.key(seed), 7)
    part_keys = jax.random.split(jax.random.fold_in(keys[6], part), 7)
    return {
        "visibility": gaussian(part_keys[0], (FREQS, 2, BASE, NT), 1.0, 6.0, ((0, 2), (2, 2), (3, 4))),
        "beam_rows": gaussian(part_keys[1], (FREQS, BASE, L), (L // 4) ** -0.5, 0.4375, ((0, 2), (1, 2))),
        "mode_gain": jnp.clip(jnp.exp(math.log(1.5) - 0.7621401 * jax.random.uniform(keys[2], (M, L), jnp.float32) ** levels(keys[2], (M, L), ((0, 4),), -0.2, 0.2)), 0.7, 1.5),
        "harmonic_basis": gaussian(keys[3], (L, L), L ** -0.5, 0.21875),
        "step_size": jnp.clip(0.15 + 0.099999994 * jax.random.uniform(part_keys[4], (FREQS,), jnp.float32) ** levels(part_keys[4], (FREQS,), ((0, 2),), -0.2, 0.2), 0.15, 0.25),
        "kl_matrix": gaussian(part_keys[5], (KEEP, FREQS), FREQS ** -0.5, 2.0),
    }


def spectral_tables(time_index, mode_index, total):
    phase = (time_index[:, None] * mode_index[None, :]) % total
    angle = phase.astype(jnp.float32) * (2.0 * jnp.pi / total)
    return jnp.cos(angle).astype(jnp.bfloat16), jnp.sin(angle).astype(jnp.bfloat16)


def reference(visibility, beam_rows, mode_gain, harmonic_basis, step_size, kl_matrix):
    nfreq = visibility.shape[0]
    nbase = visibility.shape[2]
    cosine, sine = spectral_tables(jnp.arange(NT, dtype=jnp.int32), jnp.arange(M, dtype=jnp.int32), NT)
    flat = visibility.reshape(nfreq * 2 * nbase, NT)
    first = jnp.dot(flat, cosine, preferred_element_type=jnp.float32).reshape(nfreq, 2, nbase, M)
    second = jnp.dot(flat, sine, preferred_element_type=jnp.float32).reshape(nfreq, 2, nbase, M)
    spectrum = jnp.stack([first[:, 0] + second[:, 1], first[:, 1] - second[:, 0]], axis=1) * (NT ** -0.5)
    modes = spectrum.transpose(3, 0, 1, 2).astype(jnp.bfloat16)
    mask = (jnp.arange(L)[None, :] >= jnp.arange(M)[:, None]).astype(jnp.float32)
    beam = beam_rows.astype(jnp.float32)

    def back(signal):
        summed = jnp.einsum('mfpb,fbk->mfpk', signal.astype(jnp.float32), beam)
        scaled = (summed * mode_gain[:, None, None, :]).astype(jnp.bfloat16)
        result = jnp.dot(scaled.reshape(-1, L), harmonic_basis, preferred_element_type=jnp.float32)
        return result.reshape(scaled.shape) * mask[:, None, None, :]

    def fore(coeffs):
        sampled = jnp.einsum('mfpl,kl->mfpk', coeffs.astype(jnp.float32), harmonic_basis.astype(jnp.float32))
        scaled = (sampled * mode_gain[:, None, None, :]).astype(jnp.bfloat16)
        return jnp.einsum('mfpk,fbk->mfpb', scaled.astype(jnp.float32), beam).astype(jnp.bfloat16)

    dirty = back(modes)
    stepping = step_size[None, :, None, None]
    estimate = stepping * dirty
    for counter in range(ITERS):
        rounded = estimate.astype(jnp.bfloat16)
        estimate = estimate + stepping * (dirty - back(fore(rounded)))
    rounded = estimate.astype(jnp.bfloat16)
    result = jnp.einsum('jf,mfpl->mjpl', kl_matrix.astype(jnp.float32), rounded.astype(jnp.float32))
    return result.astype(jnp.bfloat16)
```

```python
import functools
import math

import jax
import jax.numpy as jnp
import numpy as np
from jax import lax
from jax.experimental import pallas as pl
from jax.experimental.pallas import tpu as pltpu
from jax.sharding import PartitionSpec as P

NT = 8192
ITERS = 2
LANES = 128
NT_DIMS = (((1,), (1,)), ((), ()))
VMEM = pl.BlockSpec(memory_space=pltpu.VMEM)
SMEM = pl.BlockSpec(memory_space=pltpu.SMEM)


def partner_of(index, step, size):
    if size & (size - 1) == 0:
        return index ^ step, index ^ step
    return (index + step) % size, (index + size - step) % size


def exchange(array, axis, size, step):
    pairs = [(i, partner_of(i, step, size)[0]) for i in range(size)]
    return lax.ppermute(array, axis, pairs)


def phase_tables(modes, local_time, blocks):
    m = np.arange(modes, dtype=np.int64)[:, None]
    groups = local_time // LANES
    coarse = (m * np.arange(groups) * LANES) % NT
    origin = (m * np.arange(blocks) * local_time) % NT
    fine = (m * np.arange(LANES)) % NT
    unit = 2.0 * np.pi / NT
    columns = np.concatenate(
        [np.cos(coarse * unit), np.sin(coarse * unit), np.cos(origin * unit), np.sin(origin * unit)], axis=1
    )
    columns = np.pad(columns, ((0, 0), (0, -columns.shape[1] % LANES)))
    tables = (columns, np.cos(fine * unit), np.sin(fine * unit))
    return tuple(jnp.asarray(t.astype(np.float32)) for t in tables)


def transform_kernel(blocks, vis_ref, col_ref, fc_ref, fs_ref, own_ref, other_ref, cos_ref, sin_ref):
    nfreq, _, nbase, ntime = vis_ref.shape
    groups = ntime // LANES
    modes = col_ref.shape[0]
    block, part = lax.axis_index("ma"), lax.axis_index("pol")
    lane = lax.broadcasted_iota(jnp.int32, col_ref.shape, 1)
    columns = col_ref[...]
    oc = jnp.sum(jnp.where(lane == 2 * groups + block, columns, 0.0), axis=1, keepdims=True)
    os = jnp.sum(jnp.where(lane == 2 * groups + blocks + block, columns, 0.0), axis=1, keepdims=True)
    fc = fc_ref[...] * oc - fs_ref[...] * os
    fs = fs_ref[...] * oc + fc_ref[...] * os
    for u in range(groups):
        cc = columns[:, u : u + 1]
        cs = columns[:, groups + u : groups + u + 1]
        cos_ref[:, u * LANES : (u + 1) * LANES] = (cc * fc - cs * fs).astype(jnp.bfloat16)
        sin_ref[:, u * LANES : (u + 1) * LANES] = (cs * fc + cc * fs).astype(jnp.bfloat16)
    mine = vis_ref[:, part].reshape(nfreq * nbase, ntime)
    theirs = vis_ref[:, 1 - part].reshape(nfreq * nbase, ntime)
    both = jnp.concatenate([mine, theirs], axis=0)
    c = lax.dot_general(cos_ref[...], both, NT_DIMS, preferred_element_type=jnp.float32)
    s = lax.dot_general(sin_ref[...], both, NT_DIMS, preferred_element_type=jnp.float32)
    sign = (1 - 2 * part).astype(jnp.float32)
    scale = NT ** (-0.5)
    n = nfreq * nbase
    own_ref[...] = ((c[:, :n] + sign * s[:, n:]) * scale).astype(own_ref.dtype)
    other_ref[...] = ((c[:, n:] - sign * s[:, :n]) * scale).astype(other_ref.dtype)


def merge_kernel(blocks, own_ref, other_ref, *out_refs):
    rows, n = out_refs[0].shape[0], own_ref.shape[1]
    me = lax.axis_index("ma")
    for step, out_ref in enumerate(out_refs):
        to = partner_of(me, step, blocks)[0]
        at = pl.ds(pl.multiple_of(to * rows, 16), rows)
        out_ref[:, :n] = own_ref[at, :]
        out_ref[:, n:] = other_ref[at, :]


def solve_kernel(blocks, nf_blocks, *refs):
    parts = refs[:blocks]
    rows_own, rows_other, gain_ref, basis_ref, step_ref, kl_ref = refs[blocks : blocks + 6]
    terms = refs[blocks + 6 : blocks + 6 + nf_blocks]
    beam, dirty, estimate = refs[blocks + 6 + nf_blocks :]
    nfreq, nbase, degrees = rows_own.shape
    modes = gain_ref.shape[0]
    n = nfreq * nbase
    beam[:n, :] = rows_own[...].reshape(n, degrees)
    beam[n:, :] = rows_other[...].reshape(n, degrees)
    total = parts[0][...].astype(jnp.float32)
    for part in parts[1:]:
        total = total + part[...].astype(jnp.float32)
    base = (lax.broadcasted_iota(jnp.int32, (modes, 2 * n), 1) % n) // nbase
    keep = jnp.concatenate([base == f for f in range(nfreq)], axis=0)
    signal = jnp.where(keep, jnp.concatenate([total] * nfreq, axis=0), 0.0).astype(jnp.bfloat16)
    ids = lax.axis_index("ma") * modes + lax.broadcasted_iota(jnp.int32, (modes, degrees), 0)
    mask = lax.broadcasted_iota(jnp.int32, (modes, degrees), 1) >= ids

    def scaled(values):
        return jnp.concatenate(
            [(values[f * modes : (f + 1) * modes] * gain_ref[...]).astype(jnp.bfloat16) for f in range(nfreq)], axis=0
        )

    def back(signal):
        h = scaled(jnp.dot(signal, beam[...], preferred_element_type=jnp.float32))
        return jnp.dot(h, basis_ref[...], preferred_element_type=jnp.float32)

    def fore(coeffs):
        e = lax.dot_general(coeffs, basis_ref[...], NT_DIMS, preferred_element_type=jnp.float32)
        s = lax.dot_general(scaled(e), beam[...], NT_DIMS, preferred_element_type=jnp.float32)
        return jnp.where(keep, s, 0.0).astype(jnp.bfloat16)

    def rounded():
        return jnp.concatenate(
            [estimate[f * modes : (f + 1) * modes].astype(jnp.bfloat16) for f in range(nfreq)], axis=0
        )

    first = back(signal)
    for f in range(nfreq):
        at = slice(f * modes, (f + 1) * modes)
        d = jnp.where(mask, first[at], 0.0)
        dirty[at] = d
        estimate[at] = step_ref[f] * d
    for _ in range(ITERS):
        again = back(fore(rounded()))
        for f in range(nfreq):
            at = slice(f * modes, (f + 1) * modes)
            estimate[at] = estimate[at] + step_ref[f] * (dirty[at] - jnp.where(mask, again[at], 0.0))
    here = lax.axis_index("freq")
    kl = kl_ref[...].astype(jnp.float32)
    kl_row = lax.broadcasted_iota(jnp.int32, kl.shape, 0)
    kl_col = lax.broadcasted_iota(jnp.int32, kl.shape, 1)
    kept = kl.shape[0] // nf_blocks
    final = rounded().astype(jnp.float32)
    for step, out_ref in enumerate(terms):
        to = partner_of(here, step, nf_blocks)[0]
        for j in range(kept):
            acc = None
            for f in range(nfreq):
                hit = (kl_row == to * kept + j) & (kl_col == here * nfreq + f)
                weight = jnp.sum(jnp.where(hit, kl, 0.0), keepdims=True)
                term = weight * final[f * modes : (f + 1) * modes]
                acc = term if acc is None else acc + term
            out_ref[j] = acc.astype(out_ref.dtype)


def on_device(sizes, visibility, beam_rows, mode_gain, harmonic_basis, step_size, kl_matrix):
    blocks, nf_blocks = sizes["ma"], sizes["freq"]
    nfreq, _, nbase, ntime = visibility.shape
    local_modes, degrees = mode_gain.shape
    modes = local_modes * blocks
    n = nfreq * nbase
    shape = jax.ShapeDtypeStruct
    other_rows = exchange(beam_rows, "pol", 2, 1)
    columns, fc, fs = phase_tables(modes, ntime, blocks)
    own, other = pl.pallas_call(
        functools.partial(transform_kernel, blocks),
        out_shape=[shape((modes, n), jnp.bfloat16)] * 2,
        in_specs=[VMEM] * 4,
        out_specs=[VMEM] * 2,
        scratch_shapes=[pltpu.VMEM((modes, ntime), jnp.bfloat16)] * 2,
        compiler_params=pltpu.CompilerParams(vmem_limit_bytes=20 << 20),
        name="transform",
    )(visibility, columns, fc, fs)
    other = exchange(other, "pol", 2, 1)
    mine = pl.pallas_call(
        functools.partial(merge_kernel, blocks),
        out_shape=[shape((local_modes, 2 * n), jnp.bfloat16)] * blocks,
        in_specs=[VMEM] * 2,
        out_specs=[VMEM] * blocks,
        compiler_params=pltpu.CompilerParams(vmem_limit_bytes=16 << 20),
        name="merge",
    )(own, other)
    parts = [mine[0]] + [exchange(mine[k], "ma", blocks, k) for k in range(1, blocks)]
    kept = kl_matrix.shape[0] // nf_blocks
    terms = pl.pallas_call(
        functools.partial(solve_kernel, blocks, nf_blocks),
        out_shape=[shape((kept, local_modes, degrees), jnp.float32)]
        + [shape((kept, local_modes, degrees), jnp.bfloat16)] * (nf_blocks - 1),
        in_specs=[VMEM] * (blocks + 4) + [SMEM, VMEM],
        out_specs=[VMEM] * nf_blocks,
        scratch_shapes=[
            pltpu.VMEM((2 * n, degrees), jnp.bfloat16),
            pltpu.VMEM((nfreq * local_modes, degrees), jnp.float32),
            pltpu.VMEM((nfreq * local_modes, degrees), jnp.float32),
        ],
        compiler_params=pltpu.CompilerParams(vmem_limit_bytes=24 << 20),
        name="solve",
    )(*parts, beam_rows, other_rows, mode_gain, harmonic_basis, step_size, kl_matrix)
    total = terms[0]
    for k in range(1, nf_blocks):
        total = total + exchange(terms[k], "freq", nf_blocks, k).astype(jnp.float32)
    return total.astype(jnp.bfloat16).transpose(1, 0, 2)[:, :, None, :]


def solution(mesh):
    placed = (
        P(("slab", "freq"), None, "pol", "ma"),
        P(("slab", "freq"), "pol", None),
        P("ma", None),
        P(),
        P(("slab", "freq")),
        P("slab", None),
    )
    return jax.shard_map(
        functools.partial(on_device, dict(mesh.shape)),
        mesh=mesh,
        in_specs=placed,
        out_specs=P("ma", ("slab", "freq"), "pol", None),
        check_vma=False,
    )
```

```python
import functools
import math

import jax
import jax.numpy as jnp
from jax import lax
from jax.experimental import pallas as pl
from jax.experimental.pallas import tpu as pltpu
from jax.sharding import PartitionSpec as P

NT = 8192
ITERS = 2
LANES = 128
NT_DIMS = (((1,), (1,)), ((), ()))
VMEM = pl.BlockSpec(memory_space=pltpu.VMEM)


def work(microseconds):
    return pl.CostEstimate(flops=int(1e9 * microseconds), bytes_accessed=1 << 18, transcendentals=0)


def partner_of(index, step, size):
    if size & (size - 1) == 0:
        return index ^ step, index ^ step
    return (index + step) % size, (index + size - step) % size


def exchange(array, axis, size, step):
    pairs = [(i, partner_of(i, step, size)[0]) for i in range(size)]
    return lax.ppermute(array, axis, pairs)


def turn(phase):
    quarter = NT // 4
    quadrant = (phase + quarter // 2) // quarter
    angle = (phase - quadrant * quarter).astype(jnp.float32) * (2.0 * math.pi / NT)
    sq = angle * angle
    c, s = jnp.full_like(sq, 1.0 / 40320), jnp.full_like(sq, 1.0 / 362880)
    for k in (720, 24, 2):
        c = sq * -c + 1.0 / k
    c = 1.0 - sq * c
    for k in (5040, 120, 6):
        s = sq * -s + 1.0 / k
    s = angle - angle * sq * s
    swap = quadrant % 2 == 1
    cos, sin = jnp.where(swap, s, c), jnp.where(swap, c, s)
    cos = jnp.where((quadrant == 1) | (quadrant == 2), -cos, cos)
    sin = jnp.where((quadrant == 2) | (quadrant == 3), -sin, sin)
    return cos, sin


def table_kernel(ntime, cos_ref, sin_ref):
    modes = cos_ref.shape[0]
    block = lax.axis_index("ma")
    mode = lax.broadcasted_iota(jnp.int32, (modes, LANES), 0)
    lane = lax.broadcasted_iota(jnp.int32, (modes, LANES), 1)
    fc, fs = turn((mode * lane) % NT)
    cc, cs = turn((mode * (block * ntime + lane * LANES)) % NT)
    for u in range(ntime // LANES):
        at = slice(u * LANES, (u + 1) * LANES)
        c, s = cc[:, u : u + 1], cs[:, u : u + 1]
        cos_ref[:, at] = (c * fc - s * fs).astype(jnp.bfloat16)
        sin_ref[:, at] = (s * fc + c * fs).astype(jnp.bfloat16)


def transform_kernel(vis_ref, cos_ref, sin_ref, own_ref, other_ref):
    nfreq, _, nbase, ntime = vis_ref.shape
    n = nfreq * nbase
    part = lax.axis_index("pol")
    mine = vis_ref[:, part].reshape(n, ntime)
    theirs = vis_ref[:, 1 - part].reshape(n, ntime)
    both = jnp.concatenate([mine, theirs], axis=0)
    c = lax.dot_general(cos_ref[...], both, NT_DIMS, preferred_element_type=jnp.float32)
    s = lax.dot_general(sin_ref[...], both, NT_DIMS, preferred_element_type=jnp.float32)
    sign = (1 - 2 * part).astype(jnp.float32)
    scale = NT ** (-0.5)
    own_ref[...] = ((c[:, :n] + sign * s[:, n:]) * scale).astype(own_ref.dtype)
    other_ref[...] = ((c[:, n:] - sign * s[:, :n]) * scale).astype(other_ref.dtype)


def merge_kernel(blocks, own_ref, other_ref, *out_refs):
    rows, n = out_refs[0].shape[0], own_ref.shape[1]
    me = lax.axis_index("ma")
    for step, out_ref in enumerate(out_refs):
        to = partner_of(me, step, blocks)[0]
        at = pl.ds(pl.multiple_of(to * rows, 16), rows)
        out_ref[:, :n] = own_ref[at, :]
        out_ref[:, n:] = other_ref[at, :]


def solve_kernel(blocks, nf_blocks, *refs):
    parts = refs[:blocks]
    rows_own, rows_other, gain_ref, basis_ref, step_ref, kl_ref = refs[blocks : blocks + 6]
    terms = refs[blocks + 6 : blocks + 6 + nf_blocks]
    beam, dirty, estimate = refs[blocks + 6 + nf_blocks :]
    nfreq, nbase, degrees = rows_own.shape
    modes = gain_ref.shape[0]
    n = nfreq * nbase
    beam[:n, :] = rows_own[...].reshape(n, degrees)
    beam[n:, :] = rows_other[...].reshape(n, degrees)
    total = parts[0][...].astype(jnp.float32)
    for part in parts[1:]:
        total = total + part[...].astype(jnp.float32)
    base = (lax.broadcasted_iota(jnp.int32, (modes, 2 * n), 1) % n) // nbase
    keep = jnp.concatenate([base == f for f in range(nfreq)], axis=0)
    signal = jnp.where(keep, jnp.concatenate([total] * nfreq, axis=0), 0.0).astype(jnp.bfloat16)
    ids = lax.axis_index("ma") * modes + lax.broadcasted_iota(jnp.int32, (modes, degrees), 0)
    mask = lax.broadcasted_iota(jnp.int32, (modes, degrees), 1) >= ids

    def scaled(values):
        return jnp.concatenate(
            [(values[f * modes : (f + 1) * modes] * gain_ref[...]).astype(jnp.bfloat16) for f in range(nfreq)], axis=0
        )

    def back(signal):
        h = scaled(jnp.dot(signal, beam[...], preferred_element_type=jnp.float32))
        return jnp.dot(h, basis_ref[...], preferred_element_type=jnp.float32)

    def fore(coeffs):
        e = lax.dot_general(coeffs, basis_ref[...], NT_DIMS, preferred_element_type=jnp.float32)
        s = lax.dot_general(scaled(e), beam[...], NT_DIMS, preferred_element_type=jnp.float32)
        return jnp.where(keep, s, 0.0).astype(jnp.bfloat16)

    def rounded():
        return jnp.concatenate(
            [estimate[f * modes : (f + 1) * modes].astype(jnp.bfloat16) for f in range(nfreq)], axis=0
        )

    first = back(signal)
    for f in range(nfreq):
        at = slice(f * modes, (f + 1) * modes)
        d = jnp.where(mask, first[at], 0.0)
        dirty[at] = d
        estimate[at] = step_ref[:, f : f + 1] * d
    for _ in range(ITERS):
        again = back(fore(rounded()))
        for f in range(nfreq):
            at = slice(f * modes, (f + 1) * modes)
            estimate[at] = estimate[at] + step_ref[:, f : f + 1] * (dirty[at] - jnp.where(mask, again[at], 0.0))
    here = lax.axis_index("freq")
    kl = kl_ref[...].astype(jnp.float32)
    kl_row = lax.broadcasted_iota(jnp.int32, kl.shape, 0)
    kl_col = lax.broadcasted_iota(jnp.int32, kl.shape, 1)
    kept = kl.shape[0] // nf_blocks
    final = rounded().astype(jnp.float32)
    for step, out_ref in enumerate(terms):
        to = partner_of(here, step, nf_blocks)[0]
        for j in range(kept):
            acc = None
            for f in range(nfreq):
                hit = (kl_row == to * kept + j) & (kl_col == here * nfreq + f)
                weight = jnp.sum(jnp.where(hit, kl, 0.0), keepdims=True)
                term = weight * final[f * modes : (f + 1) * modes]
                acc = term if acc is None else acc + term
            out_ref[j] = acc.astype(out_ref.dtype)


def on_device(sizes, visibility, beam_rows, mode_gain, harmonic_basis, step_size, kl_matrix):
    blocks, nf_blocks = sizes["ma"], sizes["freq"]
    nfreq, _, nbase, ntime = visibility.shape
    local_modes, degrees = mode_gain.shape
    modes = local_modes * blocks
    n = nfreq * nbase
    shape = jax.ShapeDtypeStruct
    other_rows = exchange(beam_rows, "pol", 2, 1)
    cos, sin = pl.pallas_call(
        functools.partial(table_kernel, ntime),
        out_shape=[shape((modes, ntime), jnp.bfloat16)] * 2,
        out_specs=[VMEM] * 2,
        compiler_params=pltpu.CompilerParams(vmem_limit_bytes=16 << 20),
        cost_estimate=work(1.0),
        name="tables",
    )()
    own, other = pl.pallas_call(
        transform_kernel,
        out_shape=[shape((modes, n), jnp.bfloat16)] * 2,
        in_specs=[VMEM] * 3,
        out_specs=[VMEM] * 2,
        compiler_params=pltpu.CompilerParams(vmem_limit_bytes=16 << 20),
        cost_estimate=work(1.0),
        name="transform",
    )(visibility, cos, sin)
    other = exchange(other, "pol", 2, 1)
    mine = pl.pallas_call(
        functools.partial(merge_kernel, blocks),
        out_shape=[shape((local_modes, 2 * n), jnp.bfloat16)] * blocks,
        in_specs=[VMEM] * 2,
        out_specs=[VMEM] * blocks,
        compiler_params=pltpu.CompilerParams(vmem_limit_bytes=16 << 20),
        cost_estimate=work(0.1),
        name="merge",
    )(own, other)
    parts = [mine[0]] + [exchange(mine[k], "ma", blocks, k) for k in range(1, blocks)]
    kept = kl_matrix.shape[0] // nf_blocks
    terms = pl.pallas_call(
        functools.partial(solve_kernel, blocks, nf_blocks),
        out_shape=[shape((kept, local_modes, degrees), jnp.float32)]
        + [shape((kept, local_modes, degrees), jnp.bfloat16)] * (nf_blocks - 1),
        in_specs=[VMEM] * (blocks + 6),
        out_specs=[VMEM] * nf_blocks,
        scratch_shapes=[
            pltpu.VMEM((2 * n, degrees), jnp.bfloat16),
            pltpu.VMEM((nfreq * local_modes, degrees), jnp.float32),
            pltpu.VMEM((nfreq * local_modes, degrees), jnp.float32),
        ],
        compiler_params=pltpu.CompilerParams(vmem_limit_bytes=24 << 20),
        cost_estimate=work(2.5),
        name="solve",
    )(*parts, beam_rows, other_rows, mode_gain, harmonic_basis, step_size[None, :], kl_matrix)
    total = terms[0]
    for k in range(1, nf_blocks):
        total = total + exchange(terms[k], "freq", nf_blocks, k).astype(jnp.float32)
    return total.astype(jnp.bfloat16).transpose(1, 0, 2)[:, :, None, :]


def solution(mesh):
    placed = (
        P(("slab", "freq"), None, "pol", "ma"),
        P(("slab", "freq"), "pol", None),
        P("ma", None),
        P(),
        P(("slab", "freq")),
        P("slab", None),
    )
    return jax.shard_map(
        functools.partial(on_device, dict(mesh.shape)),
        mesh=mesh,
        in_specs=placed,
        out_specs=P("ma", ("slab", "freq"), "pol", None),
        check_vma=False,
    )
```

```python
import functools
import math

import jax
import jax.numpy as jnp
from jax import lax
from jax.experimental import pallas as pl
from jax.experimental.pallas import tpu as pltpu
from jax.sharding import PartitionSpec as P


NT = 8192
ITERS = 2
LANES = 128
LINE_OF_FOUR = (((0, 2), (1, 3), (2, 1), (3, 0)), ((0, 3), (1, 2), (2, 0), (3, 1)), ((0, 1), (1, 0), (2, 3), (3, 2)))
NT_DIMS = (((1,), (1,)), ((), ()))
VMEM = pl.BlockSpec(memory_space=pltpu.VMEM)


def work(microseconds):
    return pl.CostEstimate(flops=int(1e9 * microseconds), bytes_accessed=1 << 18, transcendentals=0)


def partner_of(index, step, size):
    if size & (size - 1) == 0:
        return index ^ step, index ^ step
    return (index + step) % size, (index + size - step) % size


def exchange(array, axis, size, step):
    pairs = [(i, partner_of(i, step, size)[0]) for i in range(size)]
    return lax.ppermute(array, axis, pairs)


def scatter_plan(size):
    if size == 4:
        return LINE_OF_FOUR
    return tuple(tuple((i, partner_of(i, k, size)[0]) for i in range(size)) for k in range(1, size))


def turn(phase):
    quarter = NT // 4
    quadrant = (phase + quarter // 2) // quarter
    angle = (phase - quadrant * quarter).astype(jnp.float32) * (2.0 * math.pi / NT)
    sq = angle * angle
    c, s = jnp.full_like(sq, 1.0 / 40320), jnp.full_like(sq, 1.0 / 362880)
    for k in (720, 24, 2):
        c = sq * -c + 1.0 / k
    c = 1.0 - sq * c
    for k in (5040, 120, 6):
        s = sq * -s + 1.0 / k
    s = angle - angle * sq * s
    swap = quadrant % 2 == 1
    cos, sin = jnp.where(swap, s, c), jnp.where(swap, c, s)
    cos = jnp.where((quadrant == 1) | (quadrant == 2), -cos, cos)
    sin = jnp.where((quadrant == 2) | (quadrant == 3), -sin, sin)
    return cos, sin


def table_kernel(ntime, cos_ref, sin_ref):
    modes = cos_ref.shape[0]
    block = lax.axis_index("ma")
    mode = lax.broadcasted_iota(jnp.int32, (modes, LANES), 0)
    lane = lax.broadcasted_iota(jnp.int32, (modes, LANES), 1)
    fc, fs = turn((mode * lane) % NT)
    cc, cs = turn((mode * (block * ntime + lane * LANES)) % NT)
    for u in range(ntime // LANES):
        at = slice(u * LANES, (u + 1) * LANES)
        c, s = cc[:, u : u + 1], cs[:, u : u + 1]
        cos_ref[:, at] = (c * fc - s * fs).astype(jnp.bfloat16)
        sin_ref[:, at] = (s * fc + c * fs).astype(jnp.bfloat16)


def half_of_modes(vis_ref, cos_ref, sin_ref):
    nfreq, _, nbase, ntime = vis_ref.shape
    part = lax.axis_index("pol")
    mine = vis_ref[:, part].reshape(nfreq * nbase, ntime)
    theirs = vis_ref[:, 1 - part].reshape(nfreq * nbase, ntime)
    c = lax.dot_general(cos_ref[...], mine, NT_DIMS, preferred_element_type=jnp.float32)
    s = lax.dot_general(sin_ref[...], theirs, NT_DIMS, preferred_element_type=jnp.float32)
    return (c + (1 - 2 * part).astype(jnp.float32) * s) * NT ** (-0.5)


def near_kernel(vis_ref, cos_ref, sin_ref, out_ref):
    out_ref[...] = half_of_modes(vis_ref, cos_ref, sin_ref).astype(out_ref.dtype)


def far_kernel(plan, vis_ref, cos_ref, sin_ref, near_ref, *refs):
    out_refs, far_ref = refs[:-1], refs[-1]
    far_ref[...] = half_of_modes(vis_ref, cos_ref, sin_ref).astype(far_ref.dtype)
    rows, n = out_refs[0].shape[0], near_ref.shape[1]
    me = lax.axis_index("ma")
    for pairs, out_ref in zip(((),) + plan, out_refs):
        to = me
        for source, target in pairs:
            to = jnp.where(me == source, target, to)
        at = pl.ds(pl.multiple_of(to * rows, 16), rows)
        out_ref[:, :n] = near_ref[at, :]
        out_ref[:, n:] = far_ref[at, :]


def solve_kernel(received, nf_blocks, *refs):
    blocks = received + 1
    parts = refs[:blocks]
    rows_own, rows_other, gain_ref, basis_ref, step_ref, kl_ref = refs[blocks : blocks + 6]
    terms = refs[blocks + 6 : blocks + 6 + nf_blocks]
    beam, dirty, estimate = refs[blocks + 6 + nf_blocks :]
    nfreq, nbase, degrees = rows_own.shape
    modes = gain_ref.shape[0]
    n = nfreq * nbase
    beam[:n, :] = rows_own[...].reshape(n, degrees)
    beam[n:, :] = rows_other[...].reshape(n, degrees)
    total = parts[0][...].astype(jnp.float32)
    for part in parts[1:]:
        total = total + part[...].astype(jnp.float32)
    base = (lax.broadcasted_iota(jnp.int32, (modes, 2 * n), 1) % n) // nbase
    keep = jnp.concatenate([base == f for f in range(nfreq)], axis=0)
    signal = jnp.where(keep, jnp.concatenate([total] * nfreq, axis=0), 0.0).astype(jnp.bfloat16)
    ids = lax.axis_index("ma") * modes + lax.broadcasted_iota(jnp.int32, (modes, degrees), 0)
    mask = lax.broadcasted_iota(jnp.int32, (modes, degrees), 1) >= ids

    def scaled(values):
        return jnp.concatenate(
            [(values[f * modes : (f + 1) * modes] * gain_ref[...]).astype(jnp.bfloat16) for f in range(nfreq)], axis=0
        )

    def back(signal):
        h = scaled(jnp.dot(signal, beam[...], preferred_element_type=jnp.float32))
        return jnp.dot(h, basis_ref[...], preferred_element_type=jnp.float32)

    def fore(coeffs):
        e = lax.dot_general(coeffs, basis_ref[...], NT_DIMS, preferred_element_type=jnp.float32)
        s = lax.dot_general(scaled(e), beam[...], NT_DIMS, preferred_element_type=jnp.float32)
        return jnp.where(keep, s, 0.0).astype(jnp.bfloat16)

    def rounded():
        return jnp.concatenate(
            [estimate[f * modes : (f + 1) * modes].astype(jnp.bfloat16) for f in range(nfreq)], axis=0
        )

    first = back(signal)
    for f in range(nfreq):
        at = slice(f * modes, (f + 1) * modes)
        d = jnp.where(mask, first[at], 0.0)
        dirty[at] = d
        estimate[at] = step_ref[:, f : f + 1] * d
    for _ in range(ITERS):
        again = back(fore(rounded()))
        for f in range(nfreq):
            at = slice(f * modes, (f + 1) * modes)
            estimate[at] = estimate[at] + step_ref[:, f : f + 1] * (dirty[at] - jnp.where(mask, again[at], 0.0))
    here = lax.axis_index("freq")
    kl = kl_ref[...].astype(jnp.float32)
    kl_row = lax.broadcasted_iota(jnp.int32, kl.shape, 0)
    kl_col = lax.broadcasted_iota(jnp.int32, kl.shape, 1)
    kept = kl.shape[0] // nf_blocks
    final = rounded().astype(jnp.float32)
    for step, out_ref in enumerate(terms):
        to = partner_of(here, step, nf_blocks)[0]
        for j in range(kept):
            acc = None
            for f in range(nfreq):
                hit = (kl_row == to * kept + j) & (kl_col == here * nfreq + f)
                weight = jnp.sum(jnp.where(hit, kl, 0.0), keepdims=True)
                term = weight * final[f * modes : (f + 1) * modes]
                acc = term if acc is None else acc + term
            out_ref[j] = acc.astype(out_ref.dtype)


def on_device(sizes, visibility, beam_rows, mode_gain, harmonic_basis, step_size, kl_matrix):
    blocks, nf_blocks = sizes["ma"], sizes["freq"]
    nfreq, _, nbase, ntime = visibility.shape
    local_modes, degrees = mode_gain.shape
    modes = local_modes * blocks
    n = nfreq * nbase
    shape = jax.ShapeDtypeStruct
    far_visibility = exchange(visibility, "pol", 2, 1)
    cos, sin = pl.pallas_call(
        functools.partial(table_kernel, ntime),
        out_shape=[shape((modes, ntime), jnp.bfloat16)] * 2,
        out_specs=[VMEM] * 2,
        compiler_params=pltpu.CompilerParams(vmem_limit_bytes=16 << 20),
        cost_estimate=work(1.0),
        name="tables",
    )()
    near = pl.pallas_call(
        near_kernel,
        out_shape=shape((modes, n), jnp.bfloat16),
        in_specs=[VMEM] * 3,
        out_specs=VMEM,
        compiler_params=pltpu.CompilerParams(vmem_limit_bytes=16 << 20),
        cost_estimate=work(0.5),
        name="near",
    )(visibility, cos, sin)
    plan = scatter_plan(blocks)
    mine = pl.pallas_call(
        functools.partial(far_kernel, plan),
        out_shape=[shape((local_modes, 2 * n), jnp.bfloat16)] * (len(plan) + 1),
        in_specs=[VMEM] * 4,
        out_specs=[VMEM] * (len(plan) + 1),
        scratch_shapes=[pltpu.VMEM((modes, n), jnp.bfloat16)],
        compiler_params=pltpu.CompilerParams(vmem_limit_bytes=16 << 20),
        cost_estimate=work(0.5),
        name="far",
    )(far_visibility, cos, sin, near)
    parts = [mine[0]]
    for k, pairs in enumerate(plan):
        parts.append(lax.ppermute(mine[k + 1], "ma", pairs))
    other_rows = exchange(beam_rows, "pol", 2, 1)
    kept = kl_matrix.shape[0] // nf_blocks
    terms = pl.pallas_call(
        functools.partial(solve_kernel, len(plan), nf_blocks),
        out_shape=[shape((kept, local_modes, degrees), jnp.float32)]
        + [shape((kept, local_modes, degrees), jnp.bfloat16)] * (nf_blocks - 1),
        in_specs=[VMEM] * (len(plan) + 7),
        out_specs=[VMEM] * nf_blocks,
        scratch_shapes=[
            pltpu.VMEM((2 * n, degrees), jnp.bfloat16),
            pltpu.VMEM((nfreq * local_modes, degrees), jnp.float32),
            pltpu.VMEM((nfreq * local_modes, degrees), jnp.float32),
        ],
        compiler_params=pltpu.CompilerParams(vmem_limit_bytes=24 << 20),
        cost_estimate=work(2.5),
        name="solve",
    )(*parts, beam_rows, other_rows, mode_gain, harmonic_basis, step_size[None, :], kl_matrix)
    total = terms[0]
    for k in range(1, nf_blocks):
        total = total + exchange(terms[k], "freq", nf_blocks, k).astype(jnp.float32)
    return total.astype(jnp.bfloat16).transpose(1, 0, 2)[:, :, None, :]


def solution(mesh):
    placed = (
        P(("slab", "freq"), None, "pol", "ma"),
        P(("slab", "freq"), "pol", None),
        P("ma", None),
        P(),
        P(("slab", "freq")),
        P("slab", None),
    )
    return jax.shard_map(
        functools.partial(on_device, dict(mesh.shape)),
        mesh=mesh,
        in_specs=placed,
        out_specs=P("ma", ("slab", "freq"), "pol", None),
        check_vma=False,
    )
```

```python
import functools
import math

import jax
import jax.numpy as jnp
from jax import lax
from jax.experimental import pallas as pl
from jax.experimental.pallas import tpu as pltpu
from jax.sharding import PartitionSpec as P


NT = 8192
ITERS = 2
LANES = 128
LINE_OF_FOUR = (
    (1, 5, 3, 7, 0, 4, 2, 6),
    (2, 7, 4, 5, 6, 3, 0, 1),
    (6, 3, 0, 1, 2, 7, 4, 5),
    (4, 0, 6, 2, 5, 1, 7, 3),
)
NT_DIMS = (((1,), (1,)), ((), ()))
VMEM = pl.BlockSpec(memory_space=pltpu.VMEM)


def work(microseconds):
    return pl.CostEstimate(flops=int(1e9 * microseconds), bytes_accessed=1 << 18, transcendentals=0)


def partner_of(index, step, size):
    if size & (size - 1) == 0:
        return index ^ step, index ^ step
    return (index + step) % size, (index + size - step) % size


def exchange(array, axis, size, step):
    pairs = [(i, partner_of(i, step, size)[0]) for i in range(size)]
    return lax.ppermute(array, axis, pairs)


def scatter_plan(size):
    if size == 4:
        return LINE_OF_FOUR
    return tuple(tuple(2 * partner_of(i // 2, k, size)[0] + i % 2 for i in range(2 * size)) for k in range(1, size))


def lookup(index, values):
    if len(values) * 2 > 30 or max(values) > 3:
        return sum(jnp.where(index == i, v, 0) for i, v in enumerate(values))
    return (sum(v << (2 * i) for i, v in enumerate(values)) >> (2 * index)) & 3


def turn(phase):
    quarter = NT // 4
    quadrant = (phase + quarter // 2) // quarter
    angle = (phase - quadrant * quarter).astype(jnp.float32) * (2.0 * math.pi / NT)
    sq = angle * angle
    c, s = jnp.full_like(sq, 1.0 / 40320), jnp.full_like(sq, 1.0 / 362880)
    for k in (720, 24, 2):
        c = sq * -c + 1.0 / k
    c = 1.0 - sq * c
    for k in (5040, 120, 6):
        s = sq * -s + 1.0 / k
    s = angle - angle * sq * s
    swap = quadrant % 2 == 1
    cos, sin = jnp.where(swap, s, c), jnp.where(swap, c, s)
    cos = jnp.where((quadrant == 1) | (quadrant == 2), -cos, cos)
    sin = jnp.where((quadrant == 2) | (quadrant == 3), -sin, sin)
    return cos, sin


def table_kernel(ntime, cos_ref, sin_ref):
    modes = cos_ref.shape[0]
    block = lax.axis_index("ma")
    mode = lax.broadcasted_iota(jnp.int32, (modes, LANES), 0)
    lane = lax.broadcasted_iota(jnp.int32, (modes, LANES), 1)
    fc, fs = turn((mode * lane) % NT)
    cc, cs = turn((mode * (block * ntime + lane * LANES)) % NT)
    for u in range(ntime // LANES):
        at = slice(u * LANES, (u + 1) * LANES)
        c, s = cc[:, u : u + 1], cs[:, u : u + 1]
        cos_ref[:, at] = (c * fc - s * fs).astype(jnp.bfloat16)
        sin_ref[:, at] = (s * fc + c * fs).astype(jnp.bfloat16)


def half_of_modes(vis_ref, cos_ref, sin_ref):
    nfreq, _, nbase, ntime = vis_ref.shape
    part = lax.axis_index("pol")
    mine = vis_ref[:, part].reshape(nfreq * nbase, ntime)
    theirs = vis_ref[:, 1 - part].reshape(nfreq * nbase, ntime)
    c = lax.dot_general(cos_ref[...], mine, NT_DIMS, preferred_element_type=jnp.float32)
    s = lax.dot_general(sin_ref[...], theirs, NT_DIMS, preferred_element_type=jnp.float32)
    return (c + (1 - 2 * part).astype(jnp.float32) * s) * NT ** (-0.5)


def near_kernel(vis_ref, cos_ref, sin_ref, out_ref):
    out_ref[...] = half_of_modes(vis_ref, cos_ref, sin_ref).astype(out_ref.dtype)


def far_kernel(plan, vis_ref, cos_ref, sin_ref, near_ref, *refs):
    out_refs, far_ref = refs[:-1], refs[-1]
    far_ref[...] = half_of_modes(vis_ref, cos_ref, sin_ref).astype(far_ref.dtype)
    rows, n = out_refs[0].shape[0], near_ref.shape[1]
    me = 2 * lax.axis_index("ma") + lax.axis_index("pol")
    for targets, out_ref in zip(((),) + plan, out_refs):
        to = lookup(me, [target // 2 for target in targets]) if targets else lax.axis_index("ma")
        at = pl.ds(pl.multiple_of(to * rows, 16), rows)
        out_ref[:, :n] = near_ref[at, :]
        out_ref[:, n:] = far_ref[at, :]


def prepare_kernel(rows_own, rows_other, basis_ref, beam_ref, beam_turned_ref, basis_turned_ref):
    nfreq, nbase, degrees = rows_own.shape
    n = nfreq * nbase
    beam_ref[:n, :] = rows_own[...].reshape(n, degrees)
    beam_ref[n:, :] = rows_other[...].reshape(n, degrees)
    beam_turned_ref[...] = beam_ref[...].T
    basis_turned_ref[...] = basis_ref[...].T


def solve_kernel(plan, nf_blocks, *refs):
    blocks = len(plan) + 1
    parts = refs[:blocks]
    beam, beam_turned, basis_ref, basis_turned, gain_ref, step_ref, kl_ref = refs[blocks : blocks + 7]
    terms = refs[blocks + 7 : blocks + 7 + nf_blocks]
    dirty, estimate = refs[blocks + 7 + nf_blocks :]
    modes, degrees = gain_ref.shape
    nfreq = step_ref.shape[1]
    n = beam.shape[0] // 2
    nbase = n // nfreq
    total = parts[0][...].astype(jnp.float32)
    me = 2 * lax.axis_index("ma") + lax.axis_index("pol")
    for targets, part in zip(plan, parts[1:]):
        real = [int(targets.index(i) // 2 != i // 2) for i in range(len(targets))]
        values = part[...].astype(jnp.float32)
        total = total + (values if all(real) else jnp.where(lookup(me, real) == 1, values, 0.0))
    base = (lax.broadcasted_iota(jnp.int32, (modes, 2 * n), 1) % n) // nbase
    keep = jnp.concatenate([base == f for f in range(nfreq)], axis=0)
    signal = jnp.where(keep, jnp.concatenate([total] * nfreq, axis=0), 0.0).astype(jnp.bfloat16)
    ids = lax.axis_index("ma") * modes + lax.broadcasted_iota(jnp.int32, (modes, degrees), 0)
    mask = lax.broadcasted_iota(jnp.int32, (modes, degrees), 1) >= ids

    def scaled(values):
        return jnp.concatenate(
            [(values[f * modes : (f + 1) * modes] * gain_ref[...]).astype(jnp.bfloat16) for f in range(nfreq)], axis=0
        )

    def back(signal):
        h = scaled(jnp.dot(signal, beam[...], preferred_element_type=jnp.float32))
        return jnp.dot(h, basis_ref[...], preferred_element_type=jnp.float32)

    def fore(coeffs):
        e = jnp.dot(coeffs, basis_turned[...], preferred_element_type=jnp.float32)
        s = jnp.dot(scaled(e), beam_turned[...], preferred_element_type=jnp.float32)
        return jnp.where(keep, s, 0.0).astype(jnp.bfloat16)

    def rounded():
        return jnp.concatenate(
            [estimate[f * modes : (f + 1) * modes].astype(jnp.bfloat16) for f in range(nfreq)], axis=0
        )

    first = back(signal)
    for f in range(nfreq):
        at = slice(f * modes, (f + 1) * modes)
        d = jnp.where(mask, first[at], 0.0)
        dirty[at] = d
        estimate[at] = step_ref[:, f : f + 1] * d
    for _ in range(ITERS):
        again = back(fore(rounded()))
        for f in range(nfreq):
            at = slice(f * modes, (f + 1) * modes)
            estimate[at] = estimate[at] + step_ref[:, f : f + 1] * (dirty[at] - jnp.where(mask, again[at], 0.0))
    here = lax.axis_index("freq")
    kl = kl_ref[...].astype(jnp.float32)
    kl_row = lax.broadcasted_iota(jnp.int32, kl.shape, 0)
    kl_col = lax.broadcasted_iota(jnp.int32, kl.shape, 1)
    kept = kl.shape[0] // nf_blocks
    final = rounded().astype(jnp.float32)
    for step, out_ref in enumerate(terms):
        to = partner_of(here, step, nf_blocks)[0]
        for j in range(kept):
            acc = None
            for f in range(nfreq):
                hit = (kl_row == to * kept + j) & (kl_col == here * nfreq + f)
                weight = jnp.sum(jnp.where(hit, kl, 0.0), keepdims=True)
                term = weight * final[f * modes : (f + 1) * modes]
                acc = term if acc is None else acc + term
            out_ref[j] = acc.astype(out_ref.dtype)


def on_device(sizes, visibility, beam_rows, mode_gain, harmonic_basis, step_size, kl_matrix):
    blocks, nf_blocks = sizes["ma"], sizes["freq"]
    nfreq, _, nbase, ntime = visibility.shape
    local_modes, degrees = mode_gain.shape
    modes = local_modes * blocks
    n = nfreq * nbase
    shape = jax.ShapeDtypeStruct
    far_visibility = exchange(visibility, "pol", 2, 1)
    cos, sin = pl.pallas_call(
        functools.partial(table_kernel, ntime),
        out_shape=[shape((modes, ntime), jnp.bfloat16)] * 2,
        out_specs=[VMEM] * 2,
        compiler_params=pltpu.CompilerParams(vmem_limit_bytes=16 << 20),
        cost_estimate=work(1.0),
        name="tables",
    )()
    near = pl.pallas_call(
        near_kernel,
        out_shape=shape((modes, n), jnp.bfloat16),
        in_specs=[VMEM] * 3,
        out_specs=VMEM,
        compiler_params=pltpu.CompilerParams(vmem_limit_bytes=16 << 20),
        cost_estimate=work(0.5),
        name="near",
    )(visibility, cos, sin)
    near, late_rows = lax.optimization_barrier((near, beam_rows))
    other_rows = exchange(late_rows, "pol", 2, 1)
    plan = scatter_plan(blocks)
    mine = pl.pallas_call(
        functools.partial(far_kernel, plan),
        out_shape=[shape((local_modes, 2 * n), jnp.bfloat16)] * (len(plan) + 1),
        in_specs=[VMEM] * 4,
        out_specs=[VMEM] * (len(plan) + 1),
        scratch_shapes=[pltpu.VMEM((modes, n), jnp.bfloat16)],
        compiler_params=pltpu.CompilerParams(vmem_limit_bytes=16 << 20),
        cost_estimate=work(0.5),
        name="far",
    )(far_visibility, cos, sin, near)
    parts = [mine[0]]
    for k, targets in enumerate(plan):
        parts.append(lax.ppermute(mine[k + 1], ("ma", "pol"), list(enumerate(targets))))
    tables = pl.pallas_call(
        prepare_kernel,
        out_shape=[
            shape((2 * n, degrees), jnp.bfloat16),
            shape((degrees, 2 * n), jnp.bfloat16),
            shape((degrees, degrees), jnp.bfloat16),
        ],
        in_specs=[VMEM] * 3,
        out_specs=[VMEM] * 3,
        compiler_params=pltpu.CompilerParams(vmem_limit_bytes=16 << 20),
        cost_estimate=work(0.7),
        name="prepare",
    )(beam_rows, other_rows, harmonic_basis)
    beam, beam_turned, basis_turned = tables
    kept = kl_matrix.shape[0] // nf_blocks
    terms = pl.pallas_call(
        functools.partial(solve_kernel, plan, nf_blocks),
        out_shape=[shape((kept, local_modes, degrees), jnp.float32)]
        + [shape((kept, local_modes, degrees), jnp.bfloat16)] * (nf_blocks - 1),
        in_specs=[VMEM] * (len(plan) + 8),
        out_specs=[VMEM] * nf_blocks,
        scratch_shapes=[
            pltpu.VMEM((nfreq * local_modes, degrees), jnp.float32),
            pltpu.VMEM((nfreq * local_modes, degrees), jnp.float32),
        ],
        compiler_params=pltpu.CompilerParams(vmem_limit_bytes=24 << 20),
        cost_estimate=work(2.5),
        name="solve",
    )(*parts, beam, beam_turned, harmonic_basis, basis_turned, mode_gain, step_size[None, :], kl_matrix)
    total = terms[0]
    for k in range(1, nf_blocks):
        total = total + exchange(terms[k], "freq", nf_blocks, k).astype(jnp.float32)
    return total.astype(jnp.bfloat16).transpose(1, 0, 2)[:, :, None, :]


def solution(mesh):
    placed = (
        P(("slab", "freq"), None, "pol", "ma"),
        P(("slab", "freq"), "pol", None),
        P("ma", None),
        P(),
        P(("slab", "freq")),
        P("slab", None),
    )
    return jax.shard_map(
        functools.partial(on_device, dict(mesh.shape)),
        mesh=mesh,
        in_specs=placed,
        out_specs=P("ma", ("slab", "freq"), "pol", None),
        check_vma=False,
    )
```

```python
import functools
import math

import jax
import jax.numpy as jnp
from jax import lax
from jax.experimental import pallas as pl
from jax.experimental.pallas import tpu as pltpu
from jax.sharding import PartitionSpec as P


NT = 8192
ITERS = 2
LANES = 128
LINE_OF_FOUR = (
    (1, 5, 3, 7, 0, 4, 2, 6),
    (2, 7, 4, 5, 6, 3, 0, 1),
    (6, 3, 0, 1, 2, 7, 4, 5),
    (4, 0, 6, 2, 5, 1, 7, 3),
)
NT_DIMS = (((1,), (1,)), ((), ()))
VMEM = pl.BlockSpec(memory_space=pltpu.VMEM)


def work(microseconds):
    return pl.CostEstimate(flops=int(1e9 * microseconds), bytes_accessed=1 << 18, transcendentals=0)


def partner_of(index, step, size):
    if size & (size - 1) == 0:
        return index ^ step, index ^ step
    return (index + step) % size, (index + size - step) % size


def exchange(array, axis, size, step):
    pairs = [(i, partner_of(i, step, size)[0]) for i in range(size)]
    return lax.ppermute(array, axis, pairs)


def scatter_plan(size):
    if size == 4:
        return LINE_OF_FOUR
    return tuple(tuple(2 * partner_of(i // 2, k, size)[0] + i % 2 for i in range(2 * size)) for k in range(1, size))


def lookup(index, values):
    if len(values) * 2 > 30 or max(values) > 3:
        return sum(jnp.where(index == i, v, 0) for i, v in enumerate(values))
    return (sum(v << (2 * i) for i, v in enumerate(values)) >> (2 * index)) & 3


def turn(steps):
    quarter = NT // 4
    phase = steps & (NT - 1)
    quadrant = (phase + quarter // 2) >> (quarter.bit_length() - 1)
    angle = (phase - quadrant * quarter).astype(jnp.float32) * (2.0 * math.pi / NT)
    sq = angle * angle
    c = 1.0 + sq * (-1.0 / 2 + sq * (1.0 / 24 + sq * (-1.0 / 720 + sq * (1.0 / 40320))))
    s = angle + angle * sq * (-1.0 / 6 + sq * (1.0 / 120 + sq * (-1.0 / 5040 + sq * (1.0 / 362880))))
    swap = (quadrant & 1) == 1
    cos, sin = jnp.where(swap, s, c), jnp.where(swap, c, s)
    cos = jnp.where(((quadrant + 1) & 2) == 2, -cos, cos)
    sin = jnp.where((quadrant & 2) == 2, -sin, sin)
    return cos, sin


def table_kernel(ntime, cos_ref, sin_ref):
    modes = cos_ref.shape[0]
    origin = lax.axis_index("ma") * ntime
    chunk = math.gcd(modes, 48)
    for top in range(0, modes, chunk):
        at = slice(top, top + chunk)
        mode = top + lax.broadcasted_iota(jnp.int32, (chunk, LANES), 0)
        lane = lax.broadcasted_iota(jnp.int32, (chunk, LANES), 1)
        dc, ds = turn(mode * LANES)
        c, s = turn(mode * (origin + lane))
        c_last, s_last = c * dc + s * ds, s * dc - c * ds
        for u in range(ntime // LANES):
            columns = slice(u * LANES, (u + 1) * LANES)
            cos_ref[at, columns] = c.astype(jnp.bfloat16)
            sin_ref[at, columns] = s.astype(jnp.bfloat16)
            c, c_last = (2.0 * dc) * c - c_last, c
            s, s_last = (2.0 * dc) * s - s_last, s


def half_of_modes(vis_ref, cos_ref, sin_ref):
    nfreq, _, nbase, ntime = vis_ref.shape
    part = lax.axis_index("pol")
    mine = vis_ref[:, part].reshape(nfreq * nbase, ntime)
    theirs = vis_ref[:, 1 - part].reshape(nfreq * nbase, ntime)
    c = lax.dot_general(cos_ref[...], mine, NT_DIMS, preferred_element_type=jnp.float32)
    s = lax.dot_general(sin_ref[...], theirs, NT_DIMS, preferred_element_type=jnp.float32)
    return (c + (1 - 2 * part).astype(jnp.float32) * s) * NT ** (-0.5)


def near_kernel(vis_ref, cos_ref, sin_ref, out_ref):
    out_ref[...] = half_of_modes(vis_ref, cos_ref, sin_ref).astype(out_ref.dtype)


def far_kernel(plan, vis_ref, cos_ref, sin_ref, near_ref, *refs):
    out_refs, far_ref = refs[:-1], refs[-1]
    far_ref[...] = half_of_modes(vis_ref, cos_ref, sin_ref).astype(far_ref.dtype)
    rows, n = out_refs[0].shape[0], near_ref.shape[1]
    me = 2 * lax.axis_index("ma") + lax.axis_index("pol")
    for targets, out_ref in zip(((),) + plan, out_refs):
        to = lookup(me, [target // 2 for target in targets]) if targets else lax.axis_index("ma")
        at = pl.ds(pl.multiple_of(to * rows, 16), rows)
        out_ref[:, :n] = near_ref[at, :]
        out_ref[:, n:] = far_ref[at, :]


def prepare_kernel(nf_blocks, rows_own, rows_other, basis_ref, step_ref, kl_ref, *outs):
    beam_ref, beam_turned_ref, basis_turned_ref, keep_ref, lanes_ref = outs
    nfreq, nbase, degrees = rows_own.shape
    n = nfreq * nbase
    beam_ref[:n, :] = rows_own[...].reshape(n, degrees)
    beam_ref[n:, :] = rows_other[...].reshape(n, degrees)
    beam_turned_ref[...] = beam_ref[...].T
    basis_turned_ref[...] = basis_ref[...].T
    modes = keep_ref.shape[0] // nfreq
    of_column = (lax.broadcasted_iota(jnp.int32, (modes, 2 * n), 1) % n) // nbase
    for f in range(nfreq):
        keep_ref[f * modes : (f + 1) * modes, :] = jnp.where(of_column == f, 1.0, 0.0)

    def by_column(values):
        return sum(jnp.where(of_column[:1] == f, value, 0.0) for f, value in enumerate(values))

    here = lax.axis_index("freq")
    kl = kl_ref[...].astype(jnp.float32)
    kl_row = lax.broadcasted_iota(jnp.int32, kl.shape, 0)
    kl_col = lax.broadcasted_iota(jnp.int32, kl.shape, 1)
    kept = kl.shape[0] // nf_blocks

    def weight(row, f):
        hit = (kl_row == row) & (kl_col == here * nfreq + f)
        return jnp.sum(jnp.where(hit, kl, 0.0), keepdims=True)

    lanes_ref[0:1, :] = by_column([step_ref[:, f : f + 1] for f in range(nfreq)])
    for step in range(nf_blocks):
        for j in range(kept):
            row = partner_of(here, step, nf_blocks)[0] * kept + j
            at = 1 + step * kept + j
            lanes_ref[at : at + 1, :] = by_column([weight(row, f) for f in range(nfreq)])


def solve_kernel(plan, nf_blocks, *refs):
    blocks = len(plan) + 1
    parts = refs[:blocks]
    beam, beam_turned, basis_ref, basis_turned, keep, lanes, gain_ref = refs[blocks : blocks + 7]
    terms = refs[blocks + 7 :]
    modes, degrees = gain_ref.shape
    nfreq = keep.shape[0] // modes
    total = parts[0][...].astype(jnp.float32)
    me = 2 * lax.axis_index("ma") + lax.axis_index("pol")
    for targets, part in zip(plan, parts[1:]):
        real = [int(targets.index(i) // 2 != i // 2) for i in range(len(targets))]
        values = part[...].astype(jnp.float32)
        total = total + (values if all(real) else jnp.where(lookup(me, real) == 1, values, 0.0))
    ids = lax.axis_index("ma") * modes + lax.broadcasted_iota(jnp.int32, (modes, degrees), 0)
    mask = lax.broadcasted_iota(jnp.int32, (modes, degrees), 1) >= ids

    def groups(values):
        return [values[at : at + modes] for at in range(0, values.shape[0], modes)]

    def scaled(values):
        return jnp.concatenate([(v * gain_ref[...]).astype(jnp.bfloat16) for v in groups(values)], axis=0)

    def back(signal):
        h = scaled(jnp.dot(signal, beam[...], preferred_element_type=jnp.float32))
        return [jnp.where(mask, v, 0.0) for v in groups(jnp.dot(h, basis_ref[...], preferred_element_type=jnp.float32))]

    step = lanes[0:1, :]
    y = step * total
    for _ in range(ITERS):
        spread = (jnp.concatenate([y] * nfreq, axis=0) * keep[...]).astype(jnp.bfloat16)
        coeffs = jnp.concatenate([v.astype(jnp.bfloat16) for v in back(spread)], axis=0)
        e = jnp.dot(coeffs, basis_turned[...], preferred_element_type=jnp.float32)
        again = jnp.dot(scaled(e), beam_turned[...], preferred_element_type=jnp.float32) * keep[...]
        y = y + step * (total - sum(groups(again)))
    rows = [lanes[row : row + 1, :] for row in range(1, 1 + nf_blocks * terms[0].shape[0])]
    mixed = jnp.concatenate([(y * row).astype(jnp.bfloat16) for row in rows], axis=0)
    values = back(mixed)
    for out_ref in terms:
        for j in range(out_ref.shape[0]):
            out_ref[j] = values.pop(0).astype(out_ref.dtype)


def on_device(sizes, visibility, beam_rows, mode_gain, harmonic_basis, step_size, kl_matrix):
    blocks, nf_blocks = sizes["ma"], sizes["freq"]
    nfreq, _, nbase, ntime = visibility.shape
    local_modes, degrees = mode_gain.shape
    modes = local_modes * blocks
    n = nfreq * nbase
    shape = jax.ShapeDtypeStruct
    far_visibility = exchange(visibility, "pol", 2, 1)
    cos, sin = pl.pallas_call(
        functools.partial(table_kernel, ntime),
        out_shape=[shape((modes, ntime), jnp.bfloat16)] * 2,
        out_specs=[VMEM] * 2,
        compiler_params=pltpu.CompilerParams(vmem_limit_bytes=16 << 20),
        cost_estimate=work(1.0),
        name="tables",
    )()
    near = pl.pallas_call(
        near_kernel,
        out_shape=shape((modes, n), jnp.bfloat16),
        in_specs=[VMEM] * 3,
        out_specs=VMEM,
        compiler_params=pltpu.CompilerParams(vmem_limit_bytes=16 << 20),
        cost_estimate=work(0.5),
        name="near",
    )(visibility, cos, sin)
    near, late_rows = lax.optimization_barrier((near, beam_rows))
    other_rows = exchange(late_rows, "pol", 2, 1)
    plan = scatter_plan(blocks)
    mine = pl.pallas_call(
        functools.partial(far_kernel, plan),
        out_shape=[shape((local_modes, 2 * n), jnp.bfloat16)] * (len(plan) + 1),
        in_specs=[VMEM] * 4,
        out_specs=[VMEM] * (len(plan) + 1),
        scratch_shapes=[pltpu.VMEM((modes, n), jnp.bfloat16)],
        compiler_params=pltpu.CompilerParams(vmem_limit_bytes=16 << 20),
        cost_estimate=work(0.5),
        name="far",
    )(far_visibility, cos, sin, near)
    parts = [mine[0]]
    for k, targets in enumerate(plan):
        parts.append(lax.ppermute(mine[k + 1], ("ma", "pol"), list(enumerate(targets))))
    tables = pl.pallas_call(
        functools.partial(prepare_kernel, nf_blocks),
        out_shape=[
            shape((2 * n, degrees), jnp.bfloat16),
            shape((degrees, 2 * n), jnp.bfloat16),
            shape((degrees, degrees), jnp.bfloat16),
            shape((nfreq * local_modes, 2 * n), jnp.float32),
            shape((1 + kl_matrix.shape[0], 2 * n), jnp.float32),
        ],
        in_specs=[VMEM] * 5,
        out_specs=[VMEM] * 5,
        compiler_params=pltpu.CompilerParams(vmem_limit_bytes=16 << 20),
        cost_estimate=work(0.7),
        name="prepare",
    )(beam_rows, other_rows, harmonic_basis, step_size[None, :], kl_matrix)
    beam, beam_turned, basis_turned, keep, lanes = tables
    kept = kl_matrix.shape[0] // nf_blocks
    terms = pl.pallas_call(
        functools.partial(solve_kernel, plan, nf_blocks),
        out_shape=[shape((kept, local_modes, degrees), jnp.float32)]
        + [shape((kept, local_modes, degrees), jnp.bfloat16)] * (nf_blocks - 1),
        in_specs=[VMEM] * (len(plan) + 8),
        out_specs=[VMEM] * nf_blocks,
        compiler_params=pltpu.CompilerParams(vmem_limit_bytes=24 << 20),
        cost_estimate=work(2.5),
        name="solve",
    )(*parts, beam, beam_turned, harmonic_basis, basis_turned, keep, lanes, mode_gain)
    total = terms[0]
    for k in range(1, nf_blocks):
        total = total + exchange(terms[k], "freq", nf_blocks, k).astype(jnp.float32)
    return total.astype(jnp.bfloat16).transpose(1, 0, 2)[:, :, None, :]


def solution(mesh):
    placed = (
        P(("slab", "freq"), None, "pol", "ma"),
        P(("slab", "freq"), "pol", None),
        P("ma", None),
        P(),
        P(("slab", "freq")),
        P("slab", None),
    )
    return jax.shard_map(
        functools.partial(on_device, dict(mesh.shape)),
        mesh=mesh,
        in_specs=placed,
        out_specs=P("ma", ("slab", "freq"), "pol", None),
        check_vma=False,
    )
```

```python
import functools
import math

import jax
import jax.numpy as jnp
from jax import lax
from jax.experimental import pallas as pl
from jax.experimental.pallas import tpu as pltpu
from jax.sharding import PartitionSpec as P


NT = 8192
ITERS = 2
LANES = 128
LINE_OF_FOUR = (
    (1, 5, 3, 7, 0, 4, 2, 6),
    (2, 7, 4, 5, 6, 3, 0, 1),
    (6, 3, 0, 1, 2, 7, 4, 5),
    (4, 0, 6, 2, 5, 1, 7, 3),
)
NT_DIMS = (((1,), (1,)), ((), ()))
VMEM = pl.BlockSpec(memory_space=pltpu.VMEM)


def work(microseconds):
    return pl.CostEstimate(flops=int(1e9 * microseconds), bytes_accessed=1 << 18, transcendentals=0)


def partner_of(index, step, size):
    if size & (size - 1) == 0:
        return index ^ step, index ^ step
    return (index + step) % size, (index + size - step) % size


def exchange(array, axis, size, step):
    pairs = [(i, partner_of(i, step, size)[0]) for i in range(size)]
    return lax.ppermute(array, axis, pairs)


def scatter_plan(size):
    if size == 4:
        return LINE_OF_FOUR
    return tuple(tuple(2 * partner_of(i // 2, k, size)[0] + i % 2 for i in range(2 * size)) for k in range(1, size))


def lookup(index, values):
    if len(values) * 2 > 30 or max(values) > 3:
        return sum(jnp.where(index == i, v, 0) for i, v in enumerate(values))
    return (sum(v << (2 * i) for i, v in enumerate(values)) >> (2 * index)) & 3


def turn(steps):
    quarter = NT // 4
    phase = steps & (NT - 1)
    quadrant = (phase + quarter // 2) >> (quarter.bit_length() - 1)
    angle = (phase - quadrant * quarter).astype(jnp.float32) * (2.0 * math.pi / NT)
    sq = angle * angle
    c = 1.0 + sq * (-1.0 / 2 + sq * (1.0 / 24 + sq * (-1.0 / 720 + sq * (1.0 / 40320))))
    s = angle + angle * sq * (-1.0 / 6 + sq * (1.0 / 120 + sq * (-1.0 / 5040 + sq * (1.0 / 362880))))
    swap = (quadrant & 1) == 1
    cos, sin = jnp.where(swap, s, c), jnp.where(swap, c, s)
    cos = jnp.where(((quadrant + 1) & 2) == 2, -cos, cos)
    sin = jnp.where((quadrant & 2) == 2, -sin, sin)
    return cos, sin


def table_kernel(ntime, cos_ref, sin_ref):
    modes = cos_ref.shape[0]
    origin = lax.axis_index("ma") * ntime
    chunk = math.gcd(modes, 48)
    for top in range(0, modes, chunk):
        at = slice(top, top + chunk)
        mode = top + lax.broadcasted_iota(jnp.int32, (chunk, LANES), 0)
        lane = lax.broadcasted_iota(jnp.int32, (chunk, LANES), 1)
        dc, ds = turn(mode * LANES)
        c, s = turn(mode * (origin + lane))
        c_last, s_last = c * dc + s * ds, s * dc - c * ds
        for u in range(ntime // LANES):
            columns = slice(u * LANES, (u + 1) * LANES)
            cos_ref[at, columns] = c.astype(jnp.bfloat16)
            sin_ref[at, columns] = s.astype(jnp.bfloat16)
            c, c_last = (2.0 * dc) * c - c_last, c
            s, s_last = (2.0 * dc) * s - s_last, s


def half_of_modes(vis_ref, cos_ref, sin_ref):
    nfreq, _, nbase, ntime = vis_ref.shape
    part = lax.axis_index("pol")
    mine = vis_ref[:, part].reshape(nfreq * nbase, ntime)
    theirs = vis_ref[:, 1 - part].reshape(nfreq * nbase, ntime)
    c = lax.dot_general(cos_ref[...], mine, NT_DIMS, preferred_element_type=jnp.float32)
    s = lax.dot_general(sin_ref[...], theirs, NT_DIMS, preferred_element_type=jnp.float32)
    return (c + (1 - 2 * part).astype(jnp.float32) * s) * NT ** (-0.5)


def near_kernel(vis_ref, cos_ref, sin_ref, out_ref):
    out_ref[...] = half_of_modes(vis_ref, cos_ref, sin_ref).astype(out_ref.dtype)


def far_kernel(plan, vis_ref, cos_ref, sin_ref, near_ref, *refs):
    out_refs, far_ref = refs[:-1], refs[-1]
    far_ref[...] = half_of_modes(vis_ref, cos_ref, sin_ref).astype(far_ref.dtype)
    rows, n = out_refs[0].shape[0], near_ref.shape[1]
    me = 2 * lax.axis_index("ma") + lax.axis_index("pol")
    for targets, out_ref in zip(((),) + plan, out_refs):
        to = lookup(me, [target // 2 for target in targets]) if targets else lax.axis_index("ma")
        at = pl.ds(pl.multiple_of(to * rows, 16), rows)
        out_ref[:, :n] = near_ref[at, :]
        out_ref[:, n:] = far_ref[at, :]


def prepare_kernel(nf_blocks, rows_own, rows_other, basis_ref, step_ref, kl_ref, *outs):
    beam_ref, beam_turned_ref, basis_turned_ref, keep_ref, lanes_ref = outs
    nfreq, nbase, degrees = rows_own.shape
    n = nfreq * nbase
    beam_ref[:n, :] = rows_own[...].reshape(n, degrees)
    beam_ref[n:, :] = rows_other[...].reshape(n, degrees)
    beam_turned_ref[...] = beam_ref[...].T
    basis_turned_ref[...] = basis_ref[...].T
    modes = keep_ref.shape[0] // nfreq
    of_column = (lax.broadcasted_iota(jnp.int32, (modes, 2 * n), 1) % n) // nbase
    for f in range(nfreq):
        keep_ref[f * modes : (f + 1) * modes, :] = jnp.where(of_column == f, 1.0, 0.0)

    def by_column(values):
        return sum(jnp.where(of_column[:1] == f, value, 0.0) for f, value in enumerate(values))

    here = lax.axis_index("freq")
    kl = kl_ref[...].astype(jnp.float32)
    kl_row = lax.broadcasted_iota(jnp.int32, kl.shape, 0)
    kl_col = lax.broadcasted_iota(jnp.int32, kl.shape, 1)
    kept = kl.shape[0] // nf_blocks

    def weight(row, column):
        hit = (kl_row == row) & (kl_col == column)
        return jnp.sum(jnp.where(hit, kl, 0.0), keepdims=True)

    lanes_ref[0:1, :] = by_column([step_ref[:, f : f + 1] for f in range(nfreq)])
    for step in range(nf_blocks):
        for j in range(kept):
            source = partner_of(here, step, nf_blocks)[1] * nfreq
            at = 1 + step * kept + j
            lanes_ref[at : at + 1, :] = by_column([weight(here * kept + j, source + f) for f in range(nfreq)])


def solve_kernel(plan, *refs):
    blocks = len(plan) + 1
    parts = refs[:blocks]
    beam, beam_turned, basis_ref, basis_turned, keep, lanes, gain_ref = refs[blocks : blocks + 7]
    results = refs[blocks + 7 :]
    modes, degrees = gain_ref.shape
    nfreq = keep.shape[0] // modes
    total = parts[0][...].astype(jnp.float32)
    me = 2 * lax.axis_index("ma") + lax.axis_index("pol")
    for targets, part in zip(plan, parts[1:]):
        real = [int(targets.index(i) // 2 != i // 2) for i in range(len(targets))]
        values = part[...].astype(jnp.float32)
        total = total + (values if all(real) else jnp.where(lookup(me, real) == 1, values, 0.0))
    ids = lax.axis_index("ma") * modes + lax.broadcasted_iota(jnp.int32, (modes, degrees), 0)
    mask = lax.broadcasted_iota(jnp.int32, (modes, degrees), 1) >= ids

    def groups(values):
        return [values[at : at + modes] for at in range(0, values.shape[0], modes)]

    def scaled(values):
        return jnp.concatenate([(v * gain_ref[...]).astype(jnp.bfloat16) for v in groups(values)], axis=0)

    def back(signal):
        h = scaled(jnp.dot(signal, beam[...], preferred_element_type=jnp.float32))
        return [jnp.where(mask, v, 0.0) for v in groups(jnp.dot(h, basis_ref[...], preferred_element_type=jnp.float32))]

    step = lanes[0:1, :]
    y = step * total
    for _ in range(ITERS):
        spread = (jnp.concatenate([y] * nfreq, axis=0) * keep[...]).astype(jnp.bfloat16)
        coeffs = jnp.concatenate([v.astype(jnp.bfloat16) for v in back(spread)], axis=0)
        e = jnp.dot(coeffs, basis_turned[...], preferred_element_type=jnp.float32)
        again = jnp.dot(scaled(e), beam_turned[...], preferred_element_type=jnp.float32) * keep[...]
        y = y + step * (total - sum(groups(again)))
    y_ref, mixed_ref = results
    y_ref[...] = y.astype(y_ref.dtype)
    mixed_ref[...] = mixed(y, lanes, 0, mixed_ref.shape[0] // modes)


def mixed(y, lanes, source, kept):
    first = 1 + source * kept
    return jnp.concatenate([(y * lanes[row : row + 1, :]).astype(jnp.bfloat16) for row in range(first, first + kept)], axis=0)


def near_terms_kernel(mixed_ref, beam_ref, *refs):
    *rows, sum_ref, beams_ref = refs
    sum_ref[...] = jnp.dot(mixed_ref[...], beam_ref[...], preferred_element_type=jnp.float32)
    count, width, degrees = beams_ref.shape
    for k in range(count):
        for half, ref in enumerate((rows[k], rows[count + k])):
            at = slice(half * width // 2, (half + 1) * width // 2)
            beams_ref[k, at, :] = ref[...].reshape(width // 2, degrees)


def terms_kernel(sum_ref, beams_ref, lanes_ref, gain_ref, basis_ref, *refs):
    *others, out_ref = refs
    kept, modes, degrees = out_ref.shape
    total = sum_ref[...]
    for k, y_ref in enumerate(others):
        part = mixed(y_ref[...].astype(jnp.float32), lanes_ref, k + 1, kept)
        total = total + jnp.dot(part, beams_ref[k], preferred_element_type=jnp.float32)
    ids = lax.axis_index("ma") * modes + lax.broadcasted_iota(jnp.int32, (modes, degrees), 0)
    mask = lax.broadcasted_iota(jnp.int32, (modes, degrees), 1) >= ids
    rows = [(total[j * modes : (j + 1) * modes] * gain_ref[...]).astype(jnp.bfloat16) for j in range(kept)]
    values = jnp.dot(jnp.concatenate(rows, axis=0), basis_ref[...], preferred_element_type=jnp.float32)
    for j in range(kept):
        out_ref[j] = jnp.where(mask, values[j * modes : (j + 1) * modes], 0.0).astype(out_ref.dtype)


def on_device(sizes, visibility, beam_rows, mode_gain, harmonic_basis, step_size, kl_matrix):
    blocks, nf_blocks = sizes["ma"], sizes["freq"]
    nfreq, _, nbase, ntime = visibility.shape
    local_modes, degrees = mode_gain.shape
    modes = local_modes * blocks
    n = nfreq * nbase
    shape = jax.ShapeDtypeStruct
    steps = range(1, nf_blocks)
    far_visibility = exchange(visibility, "pol", 2, 1)
    peer_rows = []
    for k in steps:
        peer_rows.append(exchange(beam_rows, "freq", nf_blocks, k))
    cos, sin = pl.pallas_call(
        functools.partial(table_kernel, ntime),
        out_shape=[shape((modes, ntime), jnp.bfloat16)] * 2,
        out_specs=[VMEM] * 2,
        compiler_params=pltpu.CompilerParams(vmem_limit_bytes=16 << 20),
        cost_estimate=work(1.0),
        name="tables",
    )()
    near = pl.pallas_call(
        near_kernel,
        out_shape=shape((modes, n), jnp.bfloat16),
        in_specs=[VMEM] * 3,
        out_specs=VMEM,
        compiler_params=pltpu.CompilerParams(vmem_limit_bytes=16 << 20),
        cost_estimate=work(0.5),
        name="near",
    )(visibility, cos, sin)
    near, late_rows = lax.optimization_barrier((near, beam_rows))
    other_rows = exchange(late_rows, "pol", 2, 1)
    plan = scatter_plan(blocks)
    mine = pl.pallas_call(
        functools.partial(far_kernel, plan),
        out_shape=[shape((local_modes, 2 * n), jnp.bfloat16)] * (len(plan) + 1),
        in_specs=[VMEM] * 4,
        out_specs=[VMEM] * (len(plan) + 1),
        scratch_shapes=[pltpu.VMEM((modes, n), jnp.bfloat16)],
        compiler_params=pltpu.CompilerParams(vmem_limit_bytes=16 << 20),
        cost_estimate=work(0.5),
        name="far",
    )(far_visibility, cos, sin, near)
    parts = [mine[0]]
    for k, targets in enumerate(plan):
        parts.append(lax.ppermute(mine[k + 1], ("ma", "pol"), list(enumerate(targets))))
    tables = pl.pallas_call(
        functools.partial(prepare_kernel, nf_blocks),
        out_shape=[
            shape((2 * n, degrees), jnp.bfloat16),
            shape((degrees, 2 * n), jnp.bfloat16),
            shape((degrees, degrees), jnp.bfloat16),
            shape((nfreq * local_modes, 2 * n), jnp.float32),
            shape((1 + kl_matrix.shape[0], 2 * n), jnp.float32),
        ],
        in_specs=[VMEM] * 5,
        out_specs=[VMEM] * 5,
        compiler_params=pltpu.CompilerParams(vmem_limit_bytes=16 << 20),
        cost_estimate=work(0.7),
        name="prepare",
    )(beam_rows, other_rows, harmonic_basis, step_size[None, :], kl_matrix)
    beam, beam_turned, basis_turned, keep, lanes = tables
    for k in steps:
        peer_rows.append(exchange(peer_rows[k - 1], "pol", 2, 1))
    kept = kl_matrix.shape[0] // nf_blocks
    y, near_mixed = pl.pallas_call(
        functools.partial(solve_kernel, plan),
        out_shape=[shape((local_modes, 2 * n), jnp.bfloat16), shape((kept * local_modes, 2 * n), jnp.bfloat16)],
        in_specs=[VMEM] * (len(plan) + 8),
        out_specs=[VMEM] * 2,
        compiler_params=pltpu.CompilerParams(vmem_limit_bytes=24 << 20),
        cost_estimate=work(2.0),
        name="solve",
    )(*parts, beam, beam_turned, harmonic_basis, basis_turned, keep, lanes, mode_gain)
    others = []
    for k in steps:
        others.append(exchange(y, "freq", nf_blocks, k))
    near_sum, beams = pl.pallas_call(
        near_terms_kernel,
        out_shape=[
            shape((kept * local_modes, degrees), jnp.float32),
            shape((nf_blocks - 1, 2 * n, degrees), jnp.bfloat16),
        ],
        in_specs=[VMEM] * (2 + len(peer_rows)),
        out_specs=[VMEM] * 2,
        compiler_params=pltpu.CompilerParams(vmem_limit_bytes=16 << 20),
        cost_estimate=work(0.5),
        name="near_terms",
    )(near_mixed, beam, *peer_rows)
    terms = pl.pallas_call(
        terms_kernel,
        out_shape=shape((kept, local_modes, degrees), jnp.bfloat16),
        in_specs=[VMEM] * (5 + len(others)),
        out_specs=VMEM,
        compiler_params=pltpu.CompilerParams(vmem_limit_bytes=16 << 20),
        cost_estimate=work(1.0),
        name="terms",
    )(near_sum, beams, lanes, mode_gain, harmonic_basis, *others)
    return terms.transpose(1, 0, 2)[:, :, None, :]


def solution(mesh):
    placed = (
        P(("slab", "freq"), None, "pol", "ma"),
        P(("slab", "freq"), "pol", None),
        P("ma", None),
        P(),
        P(("slab", "freq")),
        P("slab", None),
    )
    return jax.shard_map(
        functools.partial(on_device, dict(mesh.shape)),
        mesh=mesh,
        in_specs=placed,
        out_specs=P("ma", ("slab", "freq"), "pol", None),
        check_vma=False,
    )
```

```python
import functools
import math

import jax
import jax.numpy as jnp
from jax import lax
from jax.experimental import pallas as pl
from jax.experimental.pallas import tpu as pltpu
from jax.sharding import PartitionSpec as P


NT = 8192
ITERS = 2
LANES = 128
LINE_OF_FOUR = (
    (1, 5, 3, 2, 0, 4, 7, 6),
    (2, 7, 3, 5, 6, 4, 0, 1),
    (4, 3, 0, 7, 5, 1, 2, 6),
    (6, 0, 4, 1, 2, 3, 7, 5),
    (1, 0, 6, 2, 5, 7, 4, 3),
)
NT_DIMS = (((1,), (1,)), ((), ()))
VMEM = pl.BlockSpec(memory_space=pltpu.VMEM)


def work(microseconds):
    return pl.CostEstimate(flops=int(1e9 * microseconds), bytes_accessed=1 << 18, transcendentals=0)


def partner_of(index, step, size):
    if size & (size - 1) == 0:
        return index ^ step, index ^ step
    return (index + step) % size, (index + size - step) % size


def exchange(array, axis, size, step):
    pairs = [(i, partner_of(i, step, size)[0]) for i in range(size)]
    return lax.ppermute(array, axis, pairs)


def scatter_plan(size):
    if size == 4:
        return LINE_OF_FOUR
    return tuple(tuple(2 * partner_of(i // 2, k, size)[0] + i % 2 for i in range(2 * size)) for k in range(1, size))


def lookup(index, values):
    if len(values) * 2 > 30 or max(values) > 3:
        return sum(jnp.where(index == i, v, 0) for i, v in enumerate(values))
    return (sum(v << (2 * i) for i, v in enumerate(values)) >> (2 * index)) & 3


def turn(steps):
    quarter = NT // 4
    phase = steps & (NT - 1)
    quadrant = (phase + quarter // 2) >> (quarter.bit_length() - 1)
    angle = (phase - quadrant * quarter).astype(jnp.float32) * (2.0 * math.pi / NT)
    sq = angle * angle
    c = 1.0 + sq * (-1.0 / 2 + sq * (1.0 / 24 + sq * (-1.0 / 720 + sq * (1.0 / 40320))))
    s = angle + angle * sq * (-1.0 / 6 + sq * (1.0 / 120 + sq * (-1.0 / 5040 + sq * (1.0 / 362880))))
    swap = (quadrant & 1) == 1
    cos, sin = jnp.where(swap, s, c), jnp.where(swap, c, s)
    cos = jnp.where(((quadrant + 1) & 2) == 2, -cos, cos)
    sin = jnp.where((quadrant & 2) == 2, -sin, sin)
    return cos, sin


def table_kernel(ntime, cos_ref, sin_ref):
    modes = cos_ref.shape[0]
    origin = lax.axis_index("ma") * ntime
    chunk = math.gcd(modes, 48)
    for top in range(0, modes, chunk):
        at = slice(top, top + chunk)
        mode = top + lax.broadcasted_iota(jnp.int32, (chunk, LANES), 0)
        lane = lax.broadcasted_iota(jnp.int32, (chunk, LANES), 1)
        dc, ds = turn(mode * LANES)
        c, s = turn(mode * (origin + lane))
        c_last, s_last = c * dc + s * ds, s * dc - c * ds
        for u in range(ntime // LANES):
            columns = slice(u * LANES, (u + 1) * LANES)
            cos_ref[at, columns] = c.astype(jnp.bfloat16)
            sin_ref[at, columns] = s.astype(jnp.bfloat16)
            c, c_last = (2.0 * dc) * c - c_last, c
            s, s_last = (2.0 * dc) * s - s_last, s


def half_of_modes(vis_ref, cos_ref, sin_ref):
    nfreq, _, nbase, ntime = vis_ref.shape
    part = lax.axis_index("pol")
    mine = vis_ref[:, part].reshape(nfreq * nbase, ntime)
    theirs = vis_ref[:, 1 - part].reshape(nfreq * nbase, ntime)
    c = lax.dot_general(cos_ref[...], mine, NT_DIMS, preferred_element_type=jnp.float32)
    s = lax.dot_general(sin_ref[...], theirs, NT_DIMS, preferred_element_type=jnp.float32)
    return (c + (1 - 2 * part).astype(jnp.float32) * s) * NT ** (-0.5)


def near_kernel(vis_ref, cos_ref, sin_ref, out_ref):
    out_ref[...] = half_of_modes(vis_ref, cos_ref, sin_ref).astype(out_ref.dtype)


def far_kernel(plan, vis_ref, cos_ref, sin_ref, near_ref, *refs):
    out_refs, far_ref = refs[:-1], refs[-1]
    far_ref[...] = half_of_modes(vis_ref, cos_ref, sin_ref).astype(far_ref.dtype)
    rows, n = out_refs[0].shape[0], near_ref.shape[1]
    me = 2 * lax.axis_index("ma") + lax.axis_index("pol")
    for targets, out_ref in zip(((),) + plan, out_refs):
        to = lookup(me, [target // 2 for target in targets]) if targets else lax.axis_index("ma")
        at = pl.ds(pl.multiple_of(to * rows, 16), rows)
        out_ref[:, :n] = near_ref[at, :]
        out_ref[:, n:] = far_ref[at, :]


def prepare_kernel(nf_blocks, rows_own, rows_other, basis_ref, step_ref, kl_ref, *outs):
    beam_ref, beam_turned_ref, basis_turned_ref, keep_ref, lanes_ref = outs
    nfreq, nbase, degrees = rows_own.shape
    n = nfreq * nbase
    beam_ref[:n, :] = rows_own[...].reshape(n, degrees)
    beam_ref[n:, :] = rows_other[...].reshape(n, degrees)
    beam_turned_ref[...] = beam_ref[...].T
    basis_turned_ref[...] = basis_ref[...].T
    modes = keep_ref.shape[0] // nfreq
    of_column = (lax.broadcasted_iota(jnp.int32, (modes, 2 * n), 1) % n) // nbase
    for f in range(nfreq):
        keep_ref[f * modes : (f + 1) * modes, :] = jnp.where(of_column == f, 1.0, 0.0)

    def by_column(values):
        return sum(jnp.where(of_column[:1] == f, value, 0.0) for f, value in enumerate(values))

    here = lax.axis_index("freq")
    kl = kl_ref[...].astype(jnp.float32)
    kl_row = lax.broadcasted_iota(jnp.int32, kl.shape, 0)
    kl_col = lax.broadcasted_iota(jnp.int32, kl.shape, 1)
    kept = kl.shape[0] // nf_blocks

    def weight(row, column):
        hit = (kl_row == row) & (kl_col == column)
        return jnp.sum(jnp.where(hit, kl, 0.0), keepdims=True)

    lanes_ref[0:1, :] = by_column([step_ref[:, f : f + 1] for f in range(nfreq)])
    for step in range(nf_blocks):
        for j in range(kept):
            source = partner_of(here, step, nf_blocks)[1] * nfreq
            at = 1 + step * kept + j
            lanes_ref[at : at + 1, :] = by_column([weight(here * kept + j, source + f) for f in range(nfreq)])


def solve_kernel(plan, *refs):
    blocks = len(plan) + 1
    parts = refs[:blocks]
    beam, beam_turned, basis_ref, basis_turned, keep, lanes, gain_ref = refs[blocks : blocks + 7]
    results = refs[blocks + 7 :]
    modes, degrees = gain_ref.shape
    nfreq = keep.shape[0] // modes
    total = parts[0][...].astype(jnp.float32)
    me = 2 * lax.axis_index("ma") + lax.axis_index("pol")
    for targets, part in zip(plan, parts[1:]):
        real = [int(targets.index(i) // 2 != i // 2) for i in range(len(targets))]
        values = part[...].astype(jnp.float32)
        total = total + (values if all(real) else jnp.where(lookup(me, real) == 1, values, 0.0))
    ids = lax.axis_index("ma") * modes + lax.broadcasted_iota(jnp.int32, (modes, degrees), 0)
    mask = lax.broadcasted_iota(jnp.int32, (modes, degrees), 1) >= ids

    def groups(values):
        return [values[at : at + modes] for at in range(0, values.shape[0], modes)]

    def scaled(values):
        return jnp.concatenate([(v * gain_ref[...]).astype(jnp.bfloat16) for v in groups(values)], axis=0)

    def back(signal):
        h = scaled(jnp.dot(signal, beam[...], preferred_element_type=jnp.float32))
        return [jnp.where(mask, v, 0.0) for v in groups(jnp.dot(h, basis_ref[...], preferred_element_type=jnp.float32))]

    step = lanes[0:1, :]
    y = step * total
    for _ in range(ITERS):
        spread = (jnp.concatenate([y] * nfreq, axis=0) * keep[...]).astype(jnp.bfloat16)
        coeffs = jnp.concatenate([v.astype(jnp.bfloat16) for v in back(spread)], axis=0)
        e = jnp.dot(coeffs, basis_turned[...], preferred_element_type=jnp.float32)
        again = jnp.dot(scaled(e), beam_turned[...], preferred_element_type=jnp.float32) * keep[...]
        y = y + step * (total - sum(groups(again)))
    y_ref, mixed_ref = results
    y_ref[...] = y.astype(y_ref.dtype)
    mixed_ref[...] = mixed(y, lanes, 0, mixed_ref.shape[0] // modes)


def mixed(y, lanes, source, kept):
    first = 1 + source * kept
    return jnp.concatenate([(y * lanes[row : row + 1, :]).astype(jnp.bfloat16) for row in range(first, first + kept)], axis=0)


def near_terms_kernel(mixed_ref, beam_ref, *refs):
    *rows, sum_ref, beams_ref = refs
    sum_ref[...] = jnp.dot(mixed_ref[...], beam_ref[...], preferred_element_type=jnp.float32)
    count, width, degrees = beams_ref.shape
    for k in range(count):
        for half, ref in enumerate((rows[k], rows[count + k])):
            at = slice(half * width // 2, (half + 1) * width // 2)
            beams_ref[k, at, :] = ref[...].reshape(width // 2, degrees)


def terms_kernel(sum_ref, beams_ref, lanes_ref, gain_ref, basis_ref, *refs):
    *others, out_ref = refs
    kept, modes, degrees = out_ref.shape
    total = sum_ref[...]
    for k, y_ref in enumerate(others):
        part = mixed(y_ref[...].astype(jnp.float32), lanes_ref, k + 1, kept)
        total = total + jnp.dot(part, beams_ref[k], preferred_element_type=jnp.float32)
    ids = lax.axis_index("ma") * modes + lax.broadcasted_iota(jnp.int32, (modes, degrees), 0)
    mask = lax.broadcasted_iota(jnp.int32, (modes, degrees), 1) >= ids
    rows = [(total[j * modes : (j + 1) * modes] * gain_ref[...]).astype(jnp.bfloat16) for j in range(kept)]
    values = jnp.dot(jnp.concatenate(rows, axis=0), basis_ref[...], preferred_element_type=jnp.float32)
    for j in range(kept):
        out_ref[j] = jnp.where(mask, values[j * modes : (j + 1) * modes], 0.0).astype(out_ref.dtype)


def on_device(sizes, visibility, beam_rows, mode_gain, harmonic_basis, step_size, kl_matrix):
    blocks, nf_blocks = sizes["ma"], sizes["freq"]
    nfreq, _, nbase, ntime = visibility.shape
    local_modes, degrees = mode_gain.shape
    modes = local_modes * blocks
    n = nfreq * nbase
    shape = jax.ShapeDtypeStruct
    steps = range(1, nf_blocks)
    far_visibility = exchange(visibility, "pol", 2, 1)
    peer_rows = []
    for k in steps:
        peer_rows.append(exchange(beam_rows, "freq", nf_blocks, k))
    other_rows = exchange(beam_rows, "pol", 2, 1)
    cos, sin = pl.pallas_call(
        functools.partial(table_kernel, ntime),
        out_shape=[shape((modes, ntime), jnp.bfloat16)] * 2,
        out_specs=[VMEM] * 2,
        compiler_params=pltpu.CompilerParams(vmem_limit_bytes=16 << 20),
        cost_estimate=work(1.0),
        name="tables",
    )()
    near = pl.pallas_call(
        near_kernel,
        out_shape=shape((modes, n), jnp.bfloat16),
        in_specs=[VMEM] * 3,
        out_specs=VMEM,
        compiler_params=pltpu.CompilerParams(vmem_limit_bytes=16 << 20),
        cost_estimate=work(0.5),
        name="near",
    )(visibility, cos, sin)
    plan = scatter_plan(blocks)
    mine = pl.pallas_call(
        functools.partial(far_kernel, plan),
        out_shape=[shape((local_modes, 2 * n), jnp.bfloat16)] * (len(plan) + 1),
        in_specs=[VMEM] * 4,
        out_specs=[VMEM] * (len(plan) + 1),
        scratch_shapes=[pltpu.VMEM((modes, n), jnp.bfloat16)],
        compiler_params=pltpu.CompilerParams(vmem_limit_bytes=16 << 20),
        cost_estimate=work(0.5),
        name="far",
    )(far_visibility, cos, sin, near)
    parts = [mine[0]]
    for k, targets in enumerate(plan):
        parts.append(lax.ppermute(mine[k + 1], ("ma", "pol"), list(enumerate(targets))))
    tables = pl.pallas_call(
        functools.partial(prepare_kernel, nf_blocks),
        out_shape=[
            shape((2 * n, degrees), jnp.bfloat16),
            shape((degrees, 2 * n), jnp.bfloat16),
            shape((degrees, degrees), jnp.bfloat16),
            shape((nfreq * local_modes, 2 * n), jnp.float32),
            shape((1 + kl_matrix.shape[0], 2 * n), jnp.float32),
        ],
        in_specs=[VMEM] * 5,
        out_specs=[VMEM] * 5,
        compiler_params=pltpu.CompilerParams(vmem_limit_bytes=16 << 20),
        cost_estimate=work(0.7),
        name="prepare",
    )(beam_rows, other_rows, harmonic_basis, step_size[None, :], kl_matrix)
    beam, beam_turned, basis_turned, keep, lanes = tables
    for k in steps:
        peer_rows.append(exchange(peer_rows[k - 1], "pol", 2, 1))
    kept = kl_matrix.shape[0] // nf_blocks
    y, near_mixed = pl.pallas_call(
        functools.partial(solve_kernel, plan),
        out_shape=[shape((local_modes, 2 * n), jnp.bfloat16), shape((kept * local_modes, 2 * n), jnp.bfloat16)],
        in_specs=[VMEM] * (len(plan) + 8),
        out_specs=[VMEM] * 2,
        compiler_params=pltpu.CompilerParams(vmem_limit_bytes=24 << 20),
        cost_estimate=work(2.0),
        name="solve",
    )(*parts, beam, beam_turned, harmonic_basis, basis_turned, keep, lanes, mode_gain)
    others = []
    for k in steps:
        others.append(exchange(y, "freq", nf_blocks, k))
    near_sum, beams = pl.pallas_call(
        near_terms_kernel,
        out_shape=[
            shape((kept * local_modes, degrees), jnp.float32),
            shape((nf_blocks - 1, 2 * n, degrees), jnp.bfloat16),
        ],
        in_specs=[VMEM] * (2 + len(peer_rows)),
        out_specs=[VMEM] * 2,
        compiler_params=pltpu.CompilerParams(vmem_limit_bytes=16 << 20),
        cost_estimate=work(0.5),
        name="near_terms",
    )(near_mixed, beam, *peer_rows)
    terms = pl.pallas_call(
        terms_kernel,
        out_shape=shape((kept, local_modes, degrees), jnp.bfloat16),
        in_specs=[VMEM] * (5 + len(others)),
        out_specs=VMEM,
        compiler_params=pltpu.CompilerParams(vmem_limit_bytes=16 << 20),
        cost_estimate=work(1.0),
        name="terms",
    )(near_sum, beams, lanes, mode_gain, harmonic_basis, *others)
    return terms.transpose(1, 0, 2)[:, :, None, :]


def solution(mesh):
    placed = (
        P(("slab", "freq"), None, "pol", "ma"),
        P(("slab", "freq"), "pol", None),
        P("ma", None),
        P(),
        P(("slab", "freq")),
        P("slab", None),
    )
    return jax.shard_map(
        functools.partial(on_device, dict(mesh.shape)),
        mesh=mesh,
        in_specs=placed,
        out_specs=P("ma", ("slab", "freq"), "pol", None),
        check_vma=False,
    )
```

```python
import functools
import math

import jax
import jax.numpy as jnp
from jax import lax
from jax.experimental import pallas as pl
from jax.experimental.pallas import tpu as pltpu
from jax.sharding import PartitionSpec as P


NT = 8192
ITERS = 2
LANES = 128
LINE_OF_FOUR = (
    (1, 5, 3, 2, 0, 4, 7, 6),
    (2, 7, 3, 5, 6, 4, 0, 1),
    (4, 3, 0, 7, 5, 1, 2, 6),
    (6, 0, 4, 1, 2, 3, 7, 5),
    (1, 0, 6, 2, 5, 7, 4, 3),
)
NT_DIMS = (((1,), (1,)), ((), ()))
VMEM = pl.BlockSpec(memory_space=pltpu.VMEM)


def work(microseconds):
    return pl.CostEstimate(flops=int(1e9 * microseconds), bytes_accessed=1 << 18, transcendentals=0)


def partner_of(index, step, size):
    if size & (size - 1) == 0:
        return index ^ step, index ^ step
    return (index + step) % size, (index + size - step) % size


def exchange(array, axis, size, step):
    pairs = [(i, partner_of(i, step, size)[0]) for i in range(size)]
    return lax.ppermute(array, axis, pairs)


def scatter_plan(size):
    if size == 4:
        return LINE_OF_FOUR
    return tuple(tuple(2 * partner_of(i // 2, k, size)[0] + i % 2 for i in range(2 * size)) for k in range(1, size))


def lookup(index, values):
    if len(values) * 2 > 30 or max(values) > 3:
        return sum(jnp.where(index == i, v, 0) for i, v in enumerate(values))
    return (sum(v << (2 * i) for i, v in enumerate(values)) >> (2 * index)) & 3


def turn(steps):
    quarter = NT // 4
    phase = steps & (NT - 1)
    quadrant = (phase + quarter // 2) >> (quarter.bit_length() - 1)
    angle = (phase - quadrant * quarter).astype(jnp.float32) * (2.0 * math.pi / NT)
    sq = angle * angle
    c = 1.0 + sq * (-1.0 / 2 + sq * (1.0 / 24 + sq * (-1.0 / 720 + sq * (1.0 / 40320))))
    s = angle + angle * sq * (-1.0 / 6 + sq * (1.0 / 120 + sq * (-1.0 / 5040 + sq * (1.0 / 362880))))
    swap = (quadrant & 1) == 1
    cos, sin = jnp.where(swap, s, c), jnp.where(swap, c, s)
    cos = jnp.where(((quadrant + 1) & 2) == 2, -cos, cos)
    sin = jnp.where((quadrant & 2) == 2, -sin, sin)
    return cos, sin


def table_kernel(ntime, cos_ref, sin_ref):
    modes = cos_ref.shape[0]
    origin = lax.axis_index("ma") * ntime
    chunk = math.gcd(modes, 48)
    for top in range(0, modes, chunk):
        at = slice(top, top + chunk)
        mode = top + lax.broadcasted_iota(jnp.int32, (chunk, LANES), 0)
        lane = lax.broadcasted_iota(jnp.int32, (chunk, LANES), 1)
        dc, ds = turn(mode * LANES)
        c, s = turn(mode * (origin + lane))
        c_last, s_last = c * dc + s * ds, s * dc - c * ds
        for u in range(ntime // LANES):
            columns = slice(u * LANES, (u + 1) * LANES)
            cos_ref[at, columns] = c.astype(jnp.bfloat16)
            sin_ref[at, columns] = s.astype(jnp.bfloat16)
            c, c_last = (2.0 * dc) * c - c_last, c
            s, s_last = (2.0 * dc) * s - s_last, s


def half_of_modes(vis_ref, cos_ref, sin_ref):
    nfreq, _, nbase, ntime = vis_ref.shape
    part = lax.axis_index("pol")
    mine = vis_ref[:, part].reshape(nfreq * nbase, ntime)
    theirs = vis_ref[:, 1 - part].reshape(nfreq * nbase, ntime)
    c = lax.dot_general(cos_ref[...], mine, NT_DIMS, preferred_element_type=jnp.float32)
    s = lax.dot_general(sin_ref[...], theirs, NT_DIMS, preferred_element_type=jnp.float32)
    return (c + (1 - 2 * part).astype(jnp.float32) * s) * NT ** (-0.5)


def near_kernel(vis_ref, cos_ref, sin_ref, out_ref):
    out_ref[...] = half_of_modes(vis_ref, cos_ref, sin_ref).astype(out_ref.dtype)


def far_kernel(plan, vis_ref, cos_ref, sin_ref, near_ref, *refs):
    out_refs, far_ref = refs[:-1], refs[-1]
    rows, n = out_refs[0].shape[0], near_ref.shape[1]
    me = 2 * lax.axis_index("ma") + lax.axis_index("pol")
    places = []
    for targets, out_ref in zip(((),) + plan, out_refs):
        to = lookup(me, [target // 2 for target in targets]) if targets else lax.axis_index("ma")
        places.append(pl.ds(pl.multiple_of(to * rows, 16), rows))
        out_ref[:, :n] = near_ref[places[-1], :]
    far_ref[...] = half_of_modes(vis_ref, cos_ref, sin_ref).astype(far_ref.dtype)
    for at, out_ref in zip(places, out_refs):
        out_ref[:, n:] = far_ref[at, :]


def prepare_kernel(nf_blocks, rows_own, rows_other, basis_ref, step_ref, kl_ref, *outs):
    beam_ref, beam_turned_ref, product_ref, window_ref, keep_ref, lanes_ref = outs
    nfreq, nbase, degrees = rows_own.shape
    n = nfreq * nbase
    beam_ref[:n, :] = rows_own[...].reshape(n, degrees)
    beam_ref[n:, :] = rows_other[...].reshape(n, degrees)
    beam_turned_ref[...] = beam_ref[...].T
    modes = keep_ref.shape[0] // nfreq
    first = lax.axis_index("ma") * modes
    above = lax.broadcasted_iota(jnp.int32, basis_ref.shape, 1) >= first + modes
    shared = jnp.where(above, basis_ref[...], jnp.zeros_like(basis_ref))
    side = 2 * LANES if degrees % (2 * LANES) == 0 else degrees
    for left in range(0, degrees, side):
        columns, below = slice(left, left + side), left + side
        values = lax.dot_general(shared[:below], basis_ref[columns, :], NT_DIMS, preferred_element_type=jnp.float32)
        product_ref[:below, columns] = values.astype(jnp.bfloat16)
        for top in range(0, left, side):
            product_ref[columns, top : top + side] = values[top : top + side].T.astype(jnp.bfloat16)
    base = jnp.minimum(first // LANES * LANES, degrees - 2 * LANES)
    near = basis_ref[:, pl.ds(pl.multiple_of(base, LANES), 2 * LANES)].astype(jnp.float32)
    near = pltpu.roll(near, (2 * LANES - (first - base)) % (2 * LANES), axis=1)[:, :LANES]
    near = jnp.where(lax.broadcasted_iota(jnp.int32, near.shape, 1) < modes, near, 0.0)
    window_ref[...] = near.astype(jnp.bfloat16)
    product_ref[degrees:, :] = near.T.astype(jnp.bfloat16)
    of_column = (lax.broadcasted_iota(jnp.int32, (modes, 2 * n), 1) % n) // nbase
    for f in range(nfreq):
        keep_ref[f * modes : (f + 1) * modes, :] = jnp.where(of_column == f, 1.0, 0.0)

    def by_column(values):
        return sum(jnp.where(of_column[:1] == f, value, 0.0) for f, value in enumerate(values))

    here = lax.axis_index("freq")
    kl = kl_ref[...].astype(jnp.float32)
    kl_row = lax.broadcasted_iota(jnp.int32, kl.shape, 0)
    kl_col = lax.broadcasted_iota(jnp.int32, kl.shape, 1)
    kept = kl.shape[0] // nf_blocks

    def weight(row, column):
        hit = (kl_row == row) & (kl_col == column)
        return jnp.sum(jnp.where(hit, kl, 0.0), keepdims=True)

    lanes_ref[0:1, :] = by_column([step_ref[:, f : f + 1] for f in range(nfreq)])
    for step in range(nf_blocks):
        for j in range(kept):
            source = partner_of(here, step, nf_blocks)[1] * nfreq
            at = 1 + step * kept + j
            lanes_ref[at : at + 1, :] = by_column([weight(here * kept + j, source + f) for f in range(nfreq)])


def solve_kernel(plan, *refs):
    blocks = len(plan) + 1
    parts = refs[:blocks]
    beam, beam_turned, product, window, keep, lanes, gain_ref = refs[blocks : blocks + 7]
    results = refs[blocks + 7 :]
    modes = gain_ref.shape[0]
    nfreq = keep.shape[0] // modes
    total = parts[0][...].astype(jnp.float32)
    me = 2 * lax.axis_index("ma") + lax.axis_index("pol")
    for targets, part in zip(plan, parts[1:]):
        real = [int(targets.index(i) // 2 != i // 2) for i in range(len(targets))]
        values = part[...].astype(jnp.float32)
        total = total + (values if all(real) else jnp.where(lookup(me, real) == 1, values, 0.0))
    row = lax.broadcasted_iota(jnp.int32, (modes, LANES), 0)
    inside = lax.broadcasted_iota(jnp.int32, (modes, LANES), 1) >= row

    def groups(values):
        return [values[at : at + modes] for at in range(0, values.shape[0], modes)]

    def scaled(values):
        return jnp.concatenate([(v * gain_ref[...]).astype(jnp.bfloat16) for v in groups(values)], axis=0)

    step = lanes[0:1, :]
    y = step * total
    for _ in range(ITERS):
        spread = (jnp.concatenate([y] * nfreq, axis=0) * keep[...]).astype(jnp.bfloat16)
        h = scaled(jnp.dot(spread, beam[...], preferred_element_type=jnp.float32))
        edge = jnp.dot(h, window[...], preferred_element_type=jnp.float32)
        edge = jnp.concatenate([jnp.where(inside, v, 0.0).astype(jnp.bfloat16) for v in groups(edge)], axis=0)
        e = jnp.dot(jnp.concatenate([h, edge], axis=1), product[...], preferred_element_type=jnp.float32)
        again = jnp.dot(scaled(e), beam_turned[...], preferred_element_type=jnp.float32) * keep[...]
        y = y + step * (total - sum(groups(again)))
    (y_ref,) = results
    y_ref[...] = y.astype(y_ref.dtype)


def mixed(y, lanes, source, kept):
    first = 1 + source * kept
    return jnp.concatenate([(y * lanes[row : row + 1, :]).astype(jnp.bfloat16) for row in range(first, first + kept)], axis=0)


def near_terms_kernel(y_ref, lanes_ref, beam_ref, *refs):
    *rows, sum_ref, beams_ref = refs
    own = mixed(y_ref[...].astype(jnp.float32), lanes_ref, 0, sum_ref.shape[0] // y_ref.shape[0])
    sum_ref[...] = jnp.dot(own, beam_ref[...], preferred_element_type=jnp.float32)
    count, width, degrees = beams_ref.shape
    for k in range(count):
        for half, ref in enumerate((rows[k], rows[count + k])):
            at = slice(half * width // 2, (half + 1) * width // 2)
            beams_ref[k, at, :] = ref[...].reshape(width // 2, degrees)


def terms_kernel(sum_ref, beams_ref, lanes_ref, gain_ref, basis_ref, *refs):
    *others, out_ref = refs
    kept, modes, degrees = out_ref.shape
    total = sum_ref[...]
    for k, y_ref in enumerate(others):
        part = mixed(y_ref[...].astype(jnp.float32), lanes_ref, k + 1, kept)
        total = total + jnp.dot(part, beams_ref[k], preferred_element_type=jnp.float32)
    ids = lax.axis_index("ma") * modes + lax.broadcasted_iota(jnp.int32, (modes, degrees), 0)
    mask = lax.broadcasted_iota(jnp.int32, (modes, degrees), 1) >= ids
    rows = [(total[j * modes : (j + 1) * modes] * gain_ref[...]).astype(jnp.bfloat16) for j in range(kept)]
    values = jnp.dot(jnp.concatenate(rows, axis=0), basis_ref[...], preferred_element_type=jnp.float32)
    for j in range(kept):
        out_ref[j] = jnp.where(mask, values[j * modes : (j + 1) * modes], 0.0).astype(out_ref.dtype)


def on_device(sizes, visibility, beam_rows, mode_gain, harmonic_basis, step_size, kl_matrix):
    blocks, nf_blocks = sizes["ma"], sizes["freq"]
    nfreq, _, nbase, ntime = visibility.shape
    local_modes, degrees = mode_gain.shape
    modes = local_modes * blocks
    assert modes <= degrees and local_modes <= LANES
    n = nfreq * nbase
    shape = jax.ShapeDtypeStruct
    steps = range(1, nf_blocks)
    far_visibility = exchange(visibility, "pol", 2, 1)
    peer_rows = []
    for k in steps:
        peer_rows.append(exchange(beam_rows, "freq", nf_blocks, k))
    other_rows = exchange(beam_rows, "pol", 2, 1)
    cos, sin = pl.pallas_call(
        functools.partial(table_kernel, ntime),
        out_shape=[shape((modes, ntime), jnp.bfloat16)] * 2,
        out_specs=[VMEM] * 2,
        compiler_params=pltpu.CompilerParams(vmem_limit_bytes=16 << 20),
        cost_estimate=work(1.0),
        name="tables",
    )()
    near = pl.pallas_call(
        near_kernel,
        out_shape=shape((modes, n), jnp.bfloat16),
        in_specs=[VMEM] * 3,
        out_specs=VMEM,
        compiler_params=pltpu.CompilerParams(vmem_limit_bytes=16 << 20),
        cost_estimate=work(0.5),
        name="near",
    )(visibility, cos, sin)
    plan = scatter_plan(blocks)
    mine = pl.pallas_call(
        functools.partial(far_kernel, plan),
        out_shape=[shape((local_modes, 2 * n), jnp.bfloat16)] * (len(plan) + 1),
        in_specs=[VMEM] * 4,
        out_specs=[VMEM] * (len(plan) + 1),
        scratch_shapes=[pltpu.VMEM((modes, n), jnp.bfloat16)],
        compiler_params=pltpu.CompilerParams(vmem_limit_bytes=16 << 20),
        cost_estimate=work(0.5),
        name="far",
    )(far_visibility, cos, sin, near)
    parts = [mine[0]]
    for k, targets in enumerate(plan):
        parts.append(lax.ppermute(mine[k + 1], ("ma", "pol"), list(enumerate(targets))))
    tables = pl.pallas_call(
        functools.partial(prepare_kernel, nf_blocks),
        out_shape=[
            shape((2 * n, degrees), jnp.bfloat16),
            shape((degrees, 2 * n), jnp.bfloat16),
            shape((degrees + LANES, degrees), jnp.bfloat16),
            shape((degrees, LANES), jnp.bfloat16),
            shape((nfreq * local_modes, 2 * n), jnp.float32),
            shape((1 + kl_matrix.shape[0], 2 * n), jnp.float32),
        ],
        in_specs=[VMEM] * 5,
        out_specs=[VMEM] * 6,
        compiler_params=pltpu.CompilerParams(vmem_limit_bytes=20 << 20),
        cost_estimate=work(1.5),
        name="prepare",
    )(beam_rows, other_rows, harmonic_basis, step_size[None, :], kl_matrix)
    beam, beam_turned, product, window, keep, lanes = tables
    for k in steps:
        peer_rows.append(exchange(peer_rows[k - 1], "pol", 2, 1))
    kept = kl_matrix.shape[0] // nf_blocks
    y = pl.pallas_call(
        functools.partial(solve_kernel, plan),
        out_shape=[shape((local_modes, 2 * n), jnp.bfloat16)],
        in_specs=[VMEM] * (len(plan) + 8),
        out_specs=[VMEM],
        compiler_params=pltpu.CompilerParams(vmem_limit_bytes=24 << 20),
        cost_estimate=work(2.0),
        name="solve",
    )(*parts, beam, beam_turned, product, window, keep, lanes, mode_gain)[0]
    others = []
    for k in steps:
        others.append(exchange(y, "freq", nf_blocks, k))
    near_sum, beams = pl.pallas_call(
        near_terms_kernel,
        out_shape=[
            shape((kept * local_modes, degrees), jnp.float32),
            shape((nf_blocks - 1, 2 * n, degrees), jnp.bfloat16),
        ],
        in_specs=[VMEM] * (3 + len(peer_rows)),
        out_specs=[VMEM] * 2,
        compiler_params=pltpu.CompilerParams(vmem_limit_bytes=16 << 20),
        cost_estimate=work(0.5),
        name="near_terms",
    )(y, lanes, beam, *peer_rows)
    terms = pl.pallas_call(
        terms_kernel,
        out_shape=shape((kept, local_modes, degrees), jnp.bfloat16),
        in_specs=[VMEM] * (5 + len(others)),
        out_specs=VMEM,
        compiler_params=pltpu.CompilerParams(vmem_limit_bytes=16 << 20),
        cost_estimate=work(1.0),
        name="terms",
    )(near_sum, beams, lanes, mode_gain, harmonic_basis, *others)
    return terms.transpose(1, 0, 2)[:, :, None, :]


def solution(mesh):
    placed = (
        P(("slab", "freq"), None, "pol", "ma"),
        P(("slab", "freq"), "pol", None),
        P("ma", None),
        P(),
        P(("slab", "freq")),
        P("slab", None),
    )
    return jax.shard_map(
        functools.partial(on_device, dict(mesh.shape)),
        mesh=mesh,
        in_specs=placed,
        out_specs=P("ma", ("slab", "freq"), "pol", None),
        check_vma=False,
    )
```

```python
import functools
import math

import jax
import jax.numpy as jnp
from jax import lax
from jax.experimental import pallas as pl
from jax.experimental.pallas import tpu as pltpu
from jax.sharding import PartitionSpec as P


NT = 8192
ITERS = 2
LANES = 128
LINE_OF_FOUR = (
    (1, 5, 3, 2, 0, 4, 7, 6),
    (2, 7, 3, 5, 6, 4, 0, 1),
    (6, 3, 0, 1, 2, 7, 4, 5),
    (4, 0, 6, 7, 5, 1, 2, 3),
    (1, 0, 4, 2, 5, 3, 7, 6),
)
NT_DIMS = (((1,), (1,)), ((), ()))
VMEM = pl.BlockSpec(memory_space=pltpu.VMEM)


def work(microseconds):
    return pl.CostEstimate(flops=int(1e9 * microseconds), bytes_accessed=1 << 18, transcendentals=0)


def partner_of(index, step, size):
    if size & (size - 1) == 0:
        return index ^ step, index ^ step
    return (index + step) % size, (index + size - step) % size


def exchange(array, axis, size, step):
    pairs = [(i, partner_of(i, step, size)[0]) for i in range(size)]
    return lax.ppermute(array, axis, pairs)


def scatter_plan(size):
    if size == 4:
        return LINE_OF_FOUR
    return tuple(tuple(2 * partner_of(i // 2, k, size)[0] + i % 2 for i in range(2 * size)) for k in range(1, size))


def lookup(index, values):
    if len(values) * 2 > 30 or max(values) > 3:
        return sum(jnp.where(index == i, v, 0) for i, v in enumerate(values))
    return (sum(v << (2 * i) for i, v in enumerate(values)) >> (2 * index)) & 3


def turn(steps):
    quarter = NT // 4
    phase = steps & (NT - 1)
    quadrant = (phase + quarter // 2) >> (quarter.bit_length() - 1)
    angle = (phase - quadrant * quarter).astype(jnp.float32) * (2.0 * math.pi / NT)
    sq = angle * angle
    c = 1.0 + sq * (-1.0 / 2 + sq * (1.0 / 24 + sq * (-1.0 / 720 + sq * (1.0 / 40320))))
    s = angle + angle * sq * (-1.0 / 6 + sq * (1.0 / 120 + sq * (-1.0 / 5040 + sq * (1.0 / 362880))))
    swap = (quadrant & 1) == 1
    cos, sin = jnp.where(swap, s, c), jnp.where(swap, c, s)
    cos = jnp.where(((quadrant + 1) & 2) == 2, -cos, cos)
    sin = jnp.where((quadrant & 2) == 2, -sin, sin)
    return cos, sin


def table_kernel(ntime, cos_ref, sin_ref):
    modes = cos_ref.shape[0]
    origin = lax.axis_index("ma") * ntime
    chunk = math.gcd(modes, 48)
    for top in range(0, modes, chunk):
        at = slice(top, top + chunk)
        mode = top + lax.broadcasted_iota(jnp.int32, (chunk, LANES), 0)
        lane = lax.broadcasted_iota(jnp.int32, (chunk, LANES), 1)
        dc, ds = turn(mode * LANES)
        c, s = turn(mode * (origin + lane))
        c_last, s_last = c * dc + s * ds, s * dc - c * ds
        for u in range(ntime // LANES):
            columns = slice(u * LANES, (u + 1) * LANES)
            cos_ref[at, columns] = c.astype(jnp.bfloat16)
            sin_ref[at, columns] = s.astype(jnp.bfloat16)
            c, c_last = (2.0 * dc) * c - c_last, c
            s, s_last = (2.0 * dc) * s - s_last, s


def half_of_modes(vis_ref, cos_ref, sin_ref):
    nfreq, _, nbase, ntime = vis_ref.shape
    part = lax.axis_index("pol")
    mine = vis_ref[:, part].reshape(nfreq * nbase, ntime)
    theirs = vis_ref[:, 1 - part].reshape(nfreq * nbase, ntime)
    c = lax.dot_general(cos_ref[...], mine, NT_DIMS, preferred_element_type=jnp.float32)
    s = lax.dot_general(sin_ref[...], theirs, NT_DIMS, preferred_element_type=jnp.float32)
    return (c + (1 - 2 * part).astype(jnp.float32) * s) * NT ** (-0.5)


def near_kernel(vis_ref, cos_ref, sin_ref, out_ref):
    out_ref[...] = half_of_modes(vis_ref, cos_ref, sin_ref).astype(out_ref.dtype)


def far_kernel(plan, vis_ref, cos_ref, sin_ref, near_ref, *refs):
    out_refs, far_ref = refs[:-1], refs[-1]
    rows, n = out_refs[0].shape[0], near_ref.shape[1]
    me = 2 * lax.axis_index("ma") + lax.axis_index("pol")
    places = []
    for targets, out_ref in zip(((),) + plan, out_refs):
        to = lookup(me, [target // 2 for target in targets]) if targets else lax.axis_index("ma")
        places.append(pl.ds(pl.multiple_of(to * rows, 16), rows))
        out_ref[:, :n] = near_ref[places[-1], :]
    far_ref[...] = half_of_modes(vis_ref, cos_ref, sin_ref).astype(far_ref.dtype)
    for at, out_ref in zip(places, out_refs):
        out_ref[:, n:] = far_ref[at, :]


def prepare_kernel(nf_blocks, rows_own, rows_other, basis_ref, step_ref, kl_ref, *outs):
    beam_ref, beam_turned_ref, product_ref, window_ref, keep_ref, lanes_ref = outs
    nfreq, nbase, degrees = rows_own.shape
    n = nfreq * nbase
    beam_ref[:n, :] = rows_own[...].reshape(n, degrees)
    beam_ref[n:, :] = rows_other[...].reshape(n, degrees)
    beam_turned_ref[...] = beam_ref[...].T
    modes = keep_ref.shape[0] // nfreq
    first = lax.axis_index("ma") * modes
    above = lax.broadcasted_iota(jnp.int32, basis_ref.shape, 1) >= first + modes
    shared = jnp.where(above, basis_ref[...], jnp.zeros_like(basis_ref))
    side = 2 * LANES if degrees % (2 * LANES) == 0 else degrees
    for left in range(0, degrees, side):
        columns, below = slice(left, left + side), left + side
        values = lax.dot_general(shared[:below], basis_ref[columns, :], NT_DIMS, preferred_element_type=jnp.float32)
        product_ref[:below, columns] = values.astype(jnp.bfloat16)
        for top in range(0, left, side):
            product_ref[columns, top : top + side] = values[top : top + side].T.astype(jnp.bfloat16)
    base = jnp.minimum(first // LANES * LANES, degrees - 2 * LANES)
    near = basis_ref[:, pl.ds(pl.multiple_of(base, LANES), 2 * LANES)].astype(jnp.float32)
    near = pltpu.roll(near, (2 * LANES - (first - base)) % (2 * LANES), axis=1)[:, :LANES]
    near = jnp.where(lax.broadcasted_iota(jnp.int32, near.shape, 1) < modes, near, 0.0)
    window_ref[...] = near.astype(jnp.bfloat16)
    product_ref[degrees:, :] = near.T.astype(jnp.bfloat16)
    of_column = (lax.broadcasted_iota(jnp.int32, (modes, 2 * n), 1) % n) // nbase
    for f in range(nfreq):
        keep_ref[f * modes : (f + 1) * modes, :] = jnp.where(of_column == f, 1.0, 0.0)

    def by_column(values):
        return sum(jnp.where(of_column[:1] == f, value, 0.0) for f, value in enumerate(values))

    here = lax.axis_index("freq")
    kl = kl_ref[...].astype(jnp.float32)
    kl_row = lax.broadcasted_iota(jnp.int32, kl.shape, 0)
    kl_col = lax.broadcasted_iota(jnp.int32, kl.shape, 1)
    kept = kl.shape[0] // nf_blocks

    def weight(row, column):
        hit = (kl_row == row) & (kl_col == column)
        return jnp.sum(jnp.where(hit, kl, 0.0), keepdims=True)

    lanes_ref[0:1, :] = by_column([step_ref[:, f : f + 1] for f in range(nfreq)])
    for step in range(nf_blocks):
        for j in range(kept):
            source = partner_of(here, step, nf_blocks)[1] * nfreq
            at = 1 + step * kept + j
            lanes_ref[at : at + 1, :] = by_column([weight(here * kept + j, source + f) for f in range(nfreq)])


def solve_kernel(plan, *refs):
    blocks = len(plan) + 1
    parts = refs[:blocks]
    beam, beam_turned, product, window, keep, lanes, gain_ref = refs[blocks : blocks + 7]
    results = refs[blocks + 7 :]
    modes = gain_ref.shape[0]
    nfreq = keep.shape[0] // modes
    total = parts[0][...].astype(jnp.float32)
    me = 2 * lax.axis_index("ma") + lax.axis_index("pol")
    for targets, part in zip(plan, parts[1:]):
        real = [int(targets.index(i) // 2 != i // 2) for i in range(len(targets))]
        values = part[...].astype(jnp.float32)
        total = total + (values if all(real) else jnp.where(lookup(me, real) == 1, values, 0.0))
    row = lax.broadcasted_iota(jnp.int32, (modes, LANES), 0)
    inside = lax.broadcasted_iota(jnp.int32, (modes, LANES), 1) >= row

    def groups(values):
        return [values[at : at + modes] for at in range(0, values.shape[0], modes)]

    def scaled(values):
        return jnp.concatenate([(v * gain_ref[...]).astype(jnp.bfloat16) for v in groups(values)], axis=0)

    step = lanes[0:1, :]
    y = step * total
    for _ in range(ITERS):
        spread = (jnp.concatenate([y] * nfreq, axis=0) * keep[...]).astype(jnp.bfloat16)
        h = scaled(jnp.dot(spread, beam[...], preferred_element_type=jnp.float32))
        edge = jnp.dot(h, window[...], preferred_element_type=jnp.float32)
        edge = jnp.concatenate([jnp.where(inside, v, 0.0).astype(jnp.bfloat16) for v in groups(edge)], axis=0)
        e = jnp.dot(jnp.concatenate([h, edge], axis=1), product[...], preferred_element_type=jnp.float32)
        again = jnp.dot(scaled(e), beam_turned[...], preferred_element_type=jnp.float32) * keep[...]
        y = y + step * (total - sum(groups(again)))
    (y_ref,) = results
    y_ref[...] = y.astype(y_ref.dtype)


def mixed(y, lanes, source, kept):
    first = 1 + source * kept
    return jnp.concatenate([(y * lanes[row : row + 1, :]).astype(jnp.bfloat16) for row in range(first, first + kept)], axis=0)


def near_terms_kernel(y_ref, lanes_ref, beam_ref, *refs):
    *rows, sum_ref, beams_ref = refs
    own = mixed(y_ref[...].astype(jnp.float32), lanes_ref, 0, sum_ref.shape[0] // y_ref.shape[0])
    sum_ref[...] = jnp.dot(own, beam_ref[...], preferred_element_type=jnp.float32)
    count, width, degrees = beams_ref.shape
    for k in range(count):
        for half, ref in enumerate((rows[k], rows[count + k])):
            at = slice(half * width // 2, (half + 1) * width // 2)
            beams_ref[k, at, :] = ref[...].reshape(width // 2, degrees)


def terms_kernel(sum_ref, beams_ref, lanes_ref, gain_ref, basis_ref, *refs):
    *others, out_ref = refs
    kept, modes, degrees = out_ref.shape
    total = sum_ref[...]
    for k, y_ref in enumerate(others):
        part = mixed(y_ref[...].astype(jnp.float32), lanes_ref, k + 1, kept)
        total = total + jnp.dot(part, beams_ref[k], preferred_element_type=jnp.float32)
    ids = lax.axis_index("ma") * modes + lax.broadcasted_iota(jnp.int32, (modes, degrees), 0)
    mask = lax.broadcasted_iota(jnp.int32, (modes, degrees), 1) >= ids
    rows = [(total[j * modes : (j + 1) * modes] * gain_ref[...]).astype(jnp.bfloat16) for j in range(kept)]
    values = jnp.dot(jnp.concatenate(rows, axis=0), basis_ref[...], preferred_element_type=jnp.float32)
    for j in range(kept):
        out_ref[j] = jnp.where(mask, values[j * modes : (j + 1) * modes], 0.0).astype(out_ref.dtype)


def on_device(sizes, visibility, beam_rows, mode_gain, harmonic_basis, step_size, kl_matrix):
    blocks, nf_blocks = sizes["ma"], sizes["freq"]
    nfreq, _, nbase, ntime = visibility.shape
    local_modes, degrees = mode_gain.shape
    modes = local_modes * blocks
    assert modes <= degrees and local_modes <= LANES
    n = nfreq * nbase
    shape = jax.ShapeDtypeStruct
    steps = range(1, nf_blocks)
    far_visibility = exchange(visibility, "pol", 2, 1)
    peer_rows = []
    for k in steps:
        peer_rows.append(exchange(beam_rows, "freq", nf_blocks, k))
    other_rows = exchange(beam_rows, "pol", 2, 1)
    cos, sin = pl.pallas_call(
        functools.partial(table_kernel, ntime),
        out_shape=[shape((modes, ntime), jnp.bfloat16)] * 2,
        out_specs=[VMEM] * 2,
        compiler_params=pltpu.CompilerParams(vmem_limit_bytes=16 << 20),
        cost_estimate=work(1.0),
        name="tables",
    )()
    near = pl.pallas_call(
        near_kernel,
        out_shape=shape((modes, n), jnp.bfloat16),
        in_specs=[VMEM] * 3,
        out_specs=VMEM,
        compiler_params=pltpu.CompilerParams(vmem_limit_bytes=16 << 20),
        cost_estimate=work(0.5),
        name="near",
    )(visibility, cos, sin)
    plan = scatter_plan(blocks)
    mine = pl.pallas_call(
        functools.partial(far_kernel, plan),
        out_shape=[shape((local_modes, 2 * n), jnp.bfloat16)] * (len(plan) + 1),
        in_specs=[VMEM] * 4,
        out_specs=[VMEM] * (len(plan) + 1),
        scratch_shapes=[pltpu.VMEM((modes, n), jnp.bfloat16)],
        compiler_params=pltpu.CompilerParams(vmem_limit_bytes=16 << 20),
        cost_estimate=work(0.5),
        name="far",
    )(far_visibility, cos, sin, near)
    parts = [mine[0]]
    for k, targets in enumerate(plan):
        parts.append(lax.ppermute(mine[k + 1], ("ma", "pol"), list(enumerate(targets))))
    tables = pl.pallas_call(
        functools.partial(prepare_kernel, nf_blocks),
        out_shape=[
            shape((2 * n, degrees), jnp.bfloat16),
            shape((degrees, 2 * n), jnp.bfloat16),
            shape((degrees + LANES, degrees), jnp.bfloat16),
            shape((degrees, LANES), jnp.bfloat16),
            shape((nfreq * local_modes, 2 * n), jnp.float32),
            shape((1 + kl_matrix.shape[0], 2 * n), jnp.float32),
        ],
        in_specs=[VMEM] * 5,
        out_specs=[VMEM] * 6,
        compiler_params=pltpu.CompilerParams(vmem_limit_bytes=20 << 20),
        cost_estimate=work(1.5),
        name="prepare",
    )(beam_rows, other_rows, harmonic_basis, step_size[None, :], kl_matrix)
    beam, beam_turned, product, window, keep, lanes = tables
    for k in steps:
        peer_rows.append(exchange(peer_rows[k - 1], "pol", 2, 1))
    kept = kl_matrix.shape[0] // nf_blocks
    y = pl.pallas_call(
        functools.partial(solve_kernel, plan),
        out_shape=[shape((local_modes, 2 * n), jnp.bfloat16)],
        in_specs=[VMEM] * (len(plan) + 8),
        out_specs=[VMEM],
        compiler_params=pltpu.CompilerParams(vmem_limit_bytes=24 << 20),
        cost_estimate=work(2.0),
        name="solve",
    )(*parts, beam, beam_turned, product, window, keep, lanes, mode_gain)[0]
    others = []
    for k in steps:
        others.append(exchange(y, "freq", nf_blocks, k))
    near_sum, beams = pl.pallas_call(
        near_terms_kernel,
        out_shape=[
            shape((kept * local_modes, degrees), jnp.float32),
            shape((nf_blocks - 1, 2 * n, degrees), jnp.bfloat16),
        ],
        in_specs=[VMEM] * (3 + len(peer_rows)),
        out_specs=[VMEM] * 2,
        compiler_params=pltpu.CompilerParams(vmem_limit_bytes=16 << 20),
        cost_estimate=work(0.5),
        name="near_terms",
    )(y, lanes, beam, *peer_rows)
    terms = pl.pallas_call(
        terms_kernel,
        out_shape=shape((kept, local_modes, degrees), jnp.bfloat16),
        in_specs=[VMEM] * (5 + len(others)),
        out_specs=VMEM,
        compiler_params=pltpu.CompilerParams(vmem_limit_bytes=16 << 20),
        cost_estimate=work(1.0),
        name="terms",
    )(near_sum, beams, lanes, mode_gain, harmonic_basis, *others)
    return terms.transpose(1, 0, 2)[:, :, None, :]


def solution(mesh):
    placed = (
        P(("slab", "freq"), None, "pol", "ma"),
        P(("slab", "freq"), "pol", None),
        P("ma", None),
        P(),
        P(("slab", "freq")),
        P("slab", None),
    )
    return jax.shard_map(
        functools.partial(on_device, dict(mesh.shape)),
        mesh=mesh,
        in_specs=placed,
        out_specs=P("ma", ("slab", "freq"), "pol", None),
        check_vma=False,
    )
```
